32 devices in a mesh: scene: 2 (over y), queue: 4 (over z), tok: 2 (over x), cfg: 2 (over core).
Axes of the slice: x: 2, y: 2, z: 4, core: 2. Of those that a mesh axis runs over, the one named last changes fastest.
Arguments:
- latents: float32 [32, 16, 96], P(('scene', 'queue'), None, 'tok'), parts along dimension 0, may hold values from -6 to 6
- fresh_noise: float32 [32, 96], P(('scene', 'cfg'), 'tok'), parts along dimension 0, may hold values from -6 to 6
- levels: int32 [32], P(('scene', 'queue')), parts along dimension 0, may hold values from 0 to 15, as said below
- window_mask: int32 [32, 9], P(('scene', 'queue')), parts along dimension 0, may hold values from 0 to 1, as said below
- cond_embed: float32 [4, 1152], P(('scene', 'cfg')), parts along dimension 0, may hold values from -6 to 6
- level_mod: float32 [16, 3, 1152], replicated, may hold values from -3 to 3
- embed_weight: bfloat16 [16, 1152], replicated, may hold values from -1.5 to 1.5
- qkv_weight: bfloat16 [1152, 3, 1152], P(('queue', 'cfg'), None, 'tok'), may hold values from -0.1875 to 0.1875
- query_gain: float32 [72], replicated, may hold values from 0.25 to 1.75
- key_gain: float32 [72], replicated, may hold values from 0.25 to 1.75
- out_weight: bfloat16 [1152, 1152], P('tok', ('queue', 'cfg')), may hold values from -0.1875 to 0.1875
- final_gain: float32 [1152], replicated, may hold values from 0.5 to 1.5
- final_weight: bfloat16 [1152, 16], replicated, may hold values from -0.1875 to 0.1875
- guide_table: float32 [8], replicated, may hold values from 2 to 8
- guide_index: int32 [1], replicated, may hold values from 0 to 7
Outputs:
- velocity: float32 [32, 16, 96], P(('scene', 'queue'), 'cfg', 'tok'), parts along dimension 0
- new_queue: float32 [32, 16, 96], P(('scene', 'queue'), 'cfg', 'tok'), parts along dimension 0
The draws below stay inside these ranges and needn't reach their ends.
There are 2 independent parts, one for each index of `scene`. The reference program is written for one: setup_inputs(seed, part) draws one part's arguments, and reference() takes and returns one part's arrays. A program takes and returns all parts, laid end to end along the dimension named above; an argument that names none is the same for every part. Nothing has to cross between parts.
Inputs may be any that keep to these rules, and one draw needn't show every extreme that they name: levels[f] differs from 16 * f // 16 by at most one; the first frame has level 0 and the last 15. window_mask[f, o] = 1 lets frame f attend frame f + o - 4; window_mask[f, 4] = 1; entries whose frame lies outside 0 to 15 are 0.
All inputs are finite; a program needn't handle non-finite values.
Results may differ from the reference program's by a relative error of at most 0.0065.
Values may be sent and summed in bfloat16 or wider, within the bound.
A program may use at most 64 MiB of HBM per device.

```python
import jax
import jax.numpy as jnp
from jax import lax

D = 1152
HEADS = 16
HD = 72
C = 16
G = 8
F = 16
S = 96
LEVELS = 16
WIN = 4
HEAD_GROUP = 576
N_TOK = 2


def draw_levels(key, part):
    frame_ids = jnp.arange(F, dtype=jnp.int32)
    jitter = jax.random.randint(key, (F,), -1, 2, dtype=jnp.int32)
    base = frame_ids * LEVELS // F
    result = jnp.clip(base + jitter, 0, LEVELS - 1)
    result = jnp.where(frame_ids == 0, 0, result)
    result = jnp.where(frame_ids == F - 1, LEVELS - 1, result)
    return result.astype(jnp.int32)


def draw_window_mask(key, part):
    span = 2 * WIN + 1
    picks = jax.random.randint(key, (F, span), 0, 4, dtype=jnp.int32)
    allowed = (picks != 0).astype(jnp.int32)
    offsets = jnp.arange(span, dtype=jnp.int32)[None, :] - WIN
    target = jnp.arange(F, dtype=jnp.int32)[:, None] + offsets
    inside = (target >= 0) & (target < F)
    result = jnp.where(offsets == 0, 1, jnp.where(inside, allowed, 0))
    return result.astype(jnp.int32)


def level_of(rng, shape, cuts, low, high):
    gain, own = 1.0, jax.random.fold_in(rng, 6)
    for dim, parts in cuts:
        draws = jnp.exp(jax.random.uniform(jax.random.fold_in(own, dim), (parts,), jnp.float32, low / len(cuts), high / len(cuts)))
        gain = gain * jnp.repeat(draws, shape[dim] // parts).reshape([-1 if axis == dim else 1 for axis in range(len(shape))])
    return gain


def normal_values(key, shape, scale, most, cuts=(), kind=jnp.bfloat16):
    array = scale * jax.random.normal(key, shape, jnp.float32)
    if cuts:
        array = array * level_of(key, shape, cuts, -0.22, 0.18)
    return jnp.clip(array, -most, most).astype(kind)


def setup_inputs(seed: int = 0, part: int = 0) -> dict:
    streams_of = jax.random.split(jax.random.key(seed), 16)
    part_keys = jax.random.split(jax.random.fold_in(streams_of[15], part), 16)
    return {
        "latents": normal_values(part_keys[0], (F, C, S), 1.0, 6.0, ((0, 4), (2, 2)), jnp.float32),
        "fresh_noise": normal_values(part_keys[1], (C, S), 1.0, 6.0, ((0, 2), (1, 2)), jnp.float32),
        "levels": draw_levels(jax.random.fold_in(jax.random.fold_in(streams_of[15], part), 71), part),
        "window_mask": draw_window_mask(jax.random.fold_in(jax.random.fold_in(streams_of[15], part), 71), part),
        "cond_embed": normal_values(part_keys[4], (2, D), 1.0, 6.0, ((0, 2),), jnp.float32),
        "level_mod": normal_values(streams_of[5], (LEVELS, 3, D), 0.5, 3.0, (), jnp.float32),
        "embed_weight": normal_values(streams_of[6], (C, D), C ** -0.5, 1.5),
        "qkv_weight": normal_values(streams_of[7], (D, 3, D), D ** -0.5, 0.1875, ((0, 8), (2, 2))),
        "query_gain": jnp.clip(1.0 + 0.15 * jax.random.normal(streams_of[8], (HD,), jnp.float32), 0.25, 1.75),
        "key_gain": jnp.clip(1.0 + 0.15 * jax.random.normal(streams_of[9], (HD,), jnp.float32), 0.25, 1.75),
        "out_weight": normal_values(streams_of[10], (D, D), D ** -0.5, 0.1875, ((0, 2), (1, 8))),
        "final_gain": jnp.clip(1.0 + 0.1 * jax.random.normal(streams_of[11], (D,), jnp.float32), 0.5, 1.5),
        "final_weight": normal_values(streams_of[12], (D, C), D ** -0.5, 0.1875),
        "guide_table": jnp.clip(jax.random.uniform(streams_of[13], (G,), jnp.float32, 2.0, 8.0), 2.0, 8.0),
        "guide_index": jax.random.randint(streams_of[14], (1,), 0, G).astype(jnp.int32),
    }


EPS_NORM = 1e-06
TIME_SHIFT = 3.0

def layer_norm(values):
    center = lax.optimization_barrier(jnp.mean(values, axis=-1, keepdims=True))
    deviate = values - center
    spread = lax.optimization_barrier(jnp.mean(deviate * deviate, axis=-1, keepdims=True))
    return deviate * lax.rsqrt(spread + EPS_NORM)

def rms_norm(values, scaling):
    return values * lax.rsqrt(lax.optimization_barrier(jnp.mean(values * values, axis=-1, keepdims=True)) + EPS_NORM) * scaling

def noise_sigma(fraction):
    return TIME_SHIFT * fraction / (1.0 + (TIME_SHIFT - 1.0) * fraction)

def temporal_attention(queries, key_rows, value_rows, window_mask, first_frame, total_frames, window):
    frames = queries.shape[0]
    numerator = jnp.zeros(queries.shape, jnp.float32)
    denominator = jnp.zeros(queries.shape[:-1], jnp.float32)
    for offset in range(2 * window + 1):
        near_keys = key_rows[offset:offset + frames].astype(jnp.float32)
        near_values = value_rows[offset:offset + frames].astype(jnp.float32)
        scores = lax.optimization_barrier(jnp.sum(queries * near_keys, axis=-1)) * queries.shape[-1] ** (-0.5)
        target = first_frame + jnp.arange(frames, dtype=jnp.int32) + (offset - window)
        allowed = (window_mask[:, offset] == 1) & (target >= 0) & (target < total_frames)
        weights = jnp.exp(scores) * allowed.astype(jnp.float32)[:, None, None]
        numerator = numerator + weights[..., None] * near_values
        denominator = denominator + weights
    return numerator / denominator[..., None]

def branch_velocity(latents, levels, window_mask, cond_row, level_mod, embed_weight, qkv_weight, query_gain, key_gain, out_weight, final_gain, final_weight):
    embedded = jnp.einsum('fcs,cd->fsd', latents.astype(jnp.bfloat16).astype(jnp.float32), embed_weight.astype(jnp.float32)) + cond_row
    one_hot = (levels[:, None] == jnp.arange(LEVELS, dtype=jnp.int32)[None, :]).astype(jnp.float32)
    modulate = jnp.dot(one_hot, level_mod.reshape(LEVELS, 3 * D), precision=lax.Precision.HIGHEST).reshape(F, 3, D)
    normed = (layer_norm(embedded) * (1.0 + modulate[:, None, 1]) + modulate[:, None, 0]).astype(jnp.bfloat16)
    projected = jnp.dot(normed.reshape(F * S, D), qkv_weight.reshape(D, 3 * D), preferred_element_type=jnp.float32).reshape(F, S, 3, HEADS, HD)
    queries = rms_norm(projected[:, :, 0], query_gain)
    key_rows = rms_norm(projected[:, :, 1], key_gain).astype(jnp.bfloat16)
    value_rows = projected[:, :, 2].astype(jnp.bfloat16)
    padding = ((WIN, WIN), (0, 0), (0, 0), (0, 0))
    attended = temporal_attention(queries, jnp.pad(key_rows, padding), jnp.pad(value_rows, padding), window_mask, jnp.int32(0), F, WIN)
    attended = attended.astype(jnp.bfloat16).reshape(F * S, D)
    mixed = jnp.zeros((F * S, D), jnp.float32)
    for group_index in range(N_TOK):
        lower_edge = group_index * HEAD_GROUP
        group_term = jnp.dot(attended[:, lower_edge:lower_edge + HEAD_GROUP], out_weight[lower_edge:lower_edge + HEAD_GROUP], preferred_element_type=jnp.float32)
        mixed = mixed + group_term.astype(jnp.bfloat16).astype(jnp.float32)
    summed = embedded + modulate[:, None, 2] * mixed.reshape(F, S, D)
    final_rows = (layer_norm(summed) * final_gain).astype(jnp.bfloat16)
    result = jnp.dot(final_rows.reshape(F * S, D), final_weight, preferred_element_type=jnp.float32)
    return result.reshape(F, S, C).transpose(0, 2, 1)

def reference(latents, fresh_noise, levels, window_mask, cond_embed, level_mod, embed_weight, qkv_weight, query_gain, key_gain, out_weight, final_gain, final_weight, guide_table, guide_index):
    cond_vel = branch_velocity(latents, levels, window_mask, cond_embed[0], level_mod, embed_weight, qkv_weight, query_gain, key_gain, out_weight, final_gain, final_weight)
    uncond_vel = branch_velocity(latents, levels, window_mask, cond_embed[1], level_mod, embed_weight, qkv_weight, query_gain, key_gain, out_weight, final_gain, final_weight)
    guidance = jnp.sum(guide_table * (jnp.arange(G, dtype=jnp.int32) == guide_index[0]).astype(jnp.float32))
    velocity = uncond_vel + guidance * (cond_vel - uncond_vel)
    current = noise_sigma((levels + 1).astype(jnp.float32) / LEVELS)
    upcoming = noise_sigma(levels.astype(jnp.float32) / LEVELS)
    updated = latents + (upcoming - current)[:, None, None] * velocity
    new_queue = jnp.concatenate([updated[1:], fresh_noise[None]], axis=0)
    return (velocity, new_queue)
```

```python
import functools

import jax
import jax.numpy as jnp
from jax import lax
from jax.experimental import pallas as pl
from jax.experimental.pallas import tpu as pltpu
from jax.sharding import PartitionSpec as P

LANES = 128
HIGH = lax.Precision.HIGHEST

EPS_NORM = 1e-06
TIME_SHIFT = 3.0


def with_halo(cells, sides, width):
    for axis, dim in sides:
        count = lax.axis_size(axis)
        ends = count - 1
        head = lax.slice_in_dim(cells, 0, width, axis=dim)
        tail = lax.slice_in_dim(cells, cells.shape[dim] - width, cells.shape[dim], axis=dim)
        cells = jnp.concatenate(
            [
                lax.ppermute(tail, axis, [(i, (i + 1) % count) for i in range(ends)]),
                cells,
                lax.ppermute(head, axis, [((i + 1) % count, i) for i in range(ends)]),
            ],
            axis=dim,
        )
    return cells


def from_partner(value, axis, bit):
    return lax.ppermute(value, axis, [(i, i ^ 1 << bit) for i in range(lax.axis_size(axis))])


def shifted(value, axis, steps):
    count = lax.axis_size(axis)
    initial, last = (max(0, -steps), min(count, count - steps))
    return lax.ppermute(value, axis, [(source, source + steps) for source in range(initial, last)])


def layer_norm(values):
    center = jnp.mean(values, axis=-1, keepdims=True)
    deviate = values - center
    spread = jnp.mean(deviate * deviate, axis=-1, keepdims=True)
    return deviate * lax.rsqrt(spread + EPS_NORM)


def rms_norm(values, scaling):
    return (
        values * lax.rsqrt(jnp.mean(values * values, axis=-1, keepdims=True) + EPS_NORM) * scaling
    )


def noise_sigma(fraction):
    return TIME_SHIFT * fraction / (1.0 + (TIME_SHIFT - 1.0) * fraction)


def temporal_attention(
    queries, key_rows, value_rows, window_mask, first_frame, total_frames, window
):
    frames = queries.shape[0]
    numerator = jnp.zeros(queries.shape, jnp.float32)
    denominator = jnp.zeros(queries.shape[:-1], jnp.float32)
    for offset in range(2 * window + 1):
        near_keys = key_rows[offset : offset + frames].astype(jnp.float32)
        near_values = value_rows[offset : offset + frames].astype(jnp.float32)
        scores = jnp.sum(queries * near_keys, axis=-1) * queries.shape[-1] ** (-0.5)
        target = first_frame + jnp.arange(frames, dtype=jnp.int32) + (offset - window)
        allowed = (window_mask[:, offset] == 1) & (target >= 0) & (target < total_frames)
        weights = jnp.exp(scores) * allowed.astype(jnp.float32)[:, None, None]
        numerator = numerator + weights[..., None] * near_values
        denominator = denominator + weights
    return numerator / denominator[..., None]


def on_device_plain(
    latents,
    fresh_noise,
    levels,
    window_mask,
    cond_embed,
    level_mod,
    embed_weight,
    qkv_weight,
    query_gain,
    key_gain,
    out_weight,
    final_gain,
    final_weight,
    guide_table,
    guide_index,
):
    frames = latents.shape[0]
    tok_count = latents.shape[2]
    model_width = embed_weight.shape[1]
    head_dim = query_gain.shape[0]
    levels_all = level_mod.shape[0]
    queue_count = lax.axis_size("queue")
    all_tokens = lax.all_gather(latents, "tok", axis=2, tiled=True)
    seq_tokens = all_tokens.shape[2]
    row_count = frames * seq_tokens
    embedded = (
        jnp.einsum(
            "fcs,cd->fsd",
            all_tokens.astype(jnp.bfloat16),
            embed_weight,
            preferred_element_type=jnp.float32,
        )
        + cond_embed[0]
    )
    one_hot = (levels[:, None] == jnp.arange(levels_all, dtype=jnp.int32)[None, :]).astype(
        jnp.float32
    )
    modulate = jnp.dot(
        one_hot, level_mod.reshape(levels_all, 3 * model_width), precision=lax.Precision.HIGHEST
    ).reshape(frames, 3, model_width)
    normed = (layer_norm(embedded) * (1.0 + modulate[:, None, 1]) + modulate[:, None, 0]).astype(
        jnp.bfloat16
    )
    norm_rows = normed.reshape(row_count, model_width)
    local_cols = qkv_weight.shape[2]
    shard_piece = lax.all_gather(qkv_weight, ("queue", "cfg"), axis=0, tiled=True)
    flat_piece = shard_piece.reshape(shard_piece.shape[0], 3 * local_cols)
    projected = jnp.dot(norm_rows, flat_piece, preferred_element_type=jnp.float32)
    projected = projected.reshape(frames, seq_tokens, 3, local_cols // head_dim, head_dim)
    queries = rms_norm(projected[:, :, 0], query_gain)
    keys_values = jnp.stack(
        [
            rms_norm(projected[:, :, 1], key_gain).astype(jnp.bfloat16),
            projected[:, :, 2].astype(jnp.bfloat16),
        ]
    )
    widened = with_halo(keys_values, (("queue", 1),), frames)
    first_frame = lax.axis_index("queue") * frames
    attended = temporal_attention(
        queries, widened[0], widened[1], window_mask, first_frame, frames * queue_count, frames
    )
    attended = attended.astype(jnp.bfloat16).reshape(frames, seq_tokens, local_cols)
    flat_heads = attended.reshape(row_count, local_cols)
    partial_value = jnp.dot(
        flat_heads,
        lax.all_gather(out_weight, ("queue", "cfg"), axis=1, tiled=True),
        preferred_element_type=jnp.float32,
    )
    mixed_out = lax.psum_scatter(
        partial_value.reshape(frames, seq_tokens, model_width).astype(jnp.bfloat16),
        "tok",
        scatter_dimension=1,
        tiled=True,
    ).astype(jnp.float32)
    own_start = lax.axis_index("tok") * tok_count
    own_embed = lax.dynamic_slice_in_dim(embedded, own_start, tok_count, 1)
    summed = own_embed + modulate[:, None, 2] * mixed_out
    final_rows = (layer_norm(summed) * final_gain).astype(jnp.bfloat16)
    velocity = jnp.einsum(
        "ftd,dc->fct", final_rows, final_weight, preferred_element_type=jnp.float32
    )
    half_values = velocity.shape[1] // 2
    branch_index = lax.axis_index("cfg")
    own_first = branch_index * half_values
    other_first = (1 - branch_index) * half_values
    outgoing = lax.dynamic_slice_in_dim(velocity, other_first, half_values, 1)
    partner = from_partner(outgoing, "cfg", 0)
    mine = lax.dynamic_slice_in_dim(velocity, own_first, half_values, 1)
    is_cond = branch_index == 0
    cond_vel = jnp.where(is_cond, mine, partner)
    uncond_vel = jnp.where(is_cond, partner, mine)
    entries = guide_table.shape[0]
    guidance = jnp.sum(
        guide_table * (jnp.arange(entries, dtype=jnp.int32) == guide_index[0]).astype(jnp.float32)
    )
    guided = uncond_vel + guidance * (cond_vel - uncond_vel)
    current = noise_sigma((levels + 1).astype(jnp.float32) / levels_all)
    upcoming = noise_sigma(levels.astype(jnp.float32) / levels_all)
    own_latents = lax.dynamic_slice_in_dim(latents, own_first, half_values, 1)
    updated = own_latents + (upcoming - current)[:, None, None] * guided
    incoming = shifted(updated[:1], "queue", -1)
    is_last = lax.axis_index("queue") == queue_count - 1
    incoming = jnp.where(is_last, fresh_noise[None], incoming)
    new_queue = jnp.concatenate([updated[1:], incoming], axis=0)
    return (guided, new_queue)


def flip(index, mask):
    result, bit = index, 1
    while bit <= mask:
        if mask & bit:
            result = result + bit - 2 * bit * lax.rem(index // bit, 2)
        bit *= 2
    return result


def split2(value):
    high = value.astype(jnp.bfloat16)
    return high, (value - high.astype(jnp.float32)).astype(jnp.bfloat16)


def dot00(left, right, precision=None):
    return lax.dot_general(
        left,
        right,
        (((0,), (0,)), ((), ())),
        precision=precision,
        preferred_element_type=jnp.float32,
    )


def staged_kernel(dims, staged, plain, *refs):
    sources, rest = refs[:staged], refs[staged:]
    others, scratch = rest[: plain + 2], rest[plain + 2 :]
    holders, sems = scratch[:staged], scratch[staged]
    loads = [
        pltpu.make_async_copy(sources[i], holders[i], sems.at[i]) for i in range(staged)
    ]
    for load in loads:
        load.start()
    fused_kernel(dims, loads, *holders, *others, *scratch[staged + 1 :])


def fused_kernel(
    dims,
    loads,
    cond_ref,
    mod_ref,
    embed_ref,
    qkv_ref,
    query_gain_ref,
    key_gain_ref,
    wout_ref,
    final_gain_ref,
    wfinal_ref,
    latents_ref,
    noise_ref,
    table_ref,
    index_ref,
    levels_ref,
    mask_ref,
    guided_ref,
    queue_ref,
    cells_ref,
    wqkv_ref,
    got,
    cells,
    inputs,
    key_scale,
    value_scale,
    proj_t,
    conds,
    base,
    wq,
    wo,
    scaled_hi,
    scaled_lo,
    proj,
    q_rows,
    k_rows,
    v_rows,
    att_out,
    att_in,
    vel_half,
    vel_got,
    head_half,
    head_got,
    lat_sems,
    cond_sems,
    wq_sems,
    wqz_sems,
    wqy_sems,
    woz_sems,
    woy_sems,
    wox_sems,
    woc_sems,
    att_sems,
    end_sems,
    local_sems,
):
    nq, nt, nc, frames, chans, head_dim, window, tok_count, entries = dims
    span = 2 * window + 1
    total = nq * frames
    per_core = frames // nc
    pairs = nq * nc
    levels_all = mod_ref.shape[1]
    width = embed_ref.shape[1]
    row_level = chans + 4
    rows = cells.shape[2]
    f32, bf16 = jnp.float32, jnp.bfloat16

    s = lax.axis_index("scene")
    q = lax.axis_index("queue")
    t = lax.axis_index("tok")
    c = lax.axis_index("cfg")
    mine = q * nc + c

    barrier = pltpu.get_barrier_semaphore()
    peers = 0
    for dq in range(nq):
        for dt in range(nt):
            for dc in range(nc):
                if dq + dt + dc:
                    peers += 1
                    pl.semaphore_signal(
                        barrier,
                        inc=1,
                        device_id={
                            "queue": lax.rem(q + dq, nq),
                            "tok": lax.rem(t + dt, nt),
                            "cfg": lax.rem(c + dc, nc),
                        },
                        device_id_type=pl.DeviceIdType.MESH,
                    )
    pl.semaphore_signal(
        barrier,
        inc=1,
        device_id={"scene": 1 - s},
        device_id_type=pl.DeviceIdType.MESH,
    )
    for load in loads:
        load.wait()
    gap = LANES - 2 * tok_count
    flag_row = lax.broadcasted_iota(jnp.int32, (chans, gap), 0)
    flag_lane = lax.broadcasted_iota(jnp.int32, (chans, gap), 1)
    for i in range(frames // 2):
        flags = jnp.zeros((chans, gap), f32)
        for h in range(2):
            f = 2 * i + h
            flags = jnp.where(
                (flag_lane == h) & (flag_row == 4), levels_ref[f].astype(f32), flags
            )
            for o in range(span):
                flags = jnp.where(
                    (flag_lane == h) & (flag_row == 5 + o), mask_ref[f, o].astype(f32), flags
                )
        cells_ref[i] = jnp.concatenate(
            [latents_ref[2 * i], latents_ref[2 * i + 1], flags], axis=1
        ).astype(bf16)
    packed = wqkv_ref.shape[2]
    empty = jnp.zeros((qkv_ref.shape[1], packed - 3 * head_dim), f32)
    thirds = [qkv_ref[i].astype(f32) for i in range(3)]
    for j in range(pairs):
        cut = [part[:, j * head_dim : (j + 1) * head_dim] for part in thirds]
        wqkv_ref[j] = jnp.concatenate([*cut, empty], axis=1).astype(bf16)
    inputs[...] = jnp.zeros(inputs.shape, bf16)
    pl.semaphore_wait(barrier, peers + 1)

    def remote(source, target, sems, place, dq, dt, dc, ds=0):
        return pltpu.make_async_remote_copy(
            src_ref=source,
            dst_ref=target,
            send_sem=sems.at[(0, *place)],
            recv_sem=sems.at[(1, *place)],
            device_id={
                "scene": lax.rem(s + ds, 2),
                "queue": lax.rem(q + dq, nq),
                "tok": lax.rem(t + dt, nt),
                "cfg": lax.rem(c + dc, nc),
            },
            device_id_type=pl.DeviceIdType.MESH,
        )

    own_cells = got.at[t, pl.ds(q * (frames // 2), frames // 2)]
    lat_copies = [
        remote(cells_ref, own_cells, lat_sems, (dq, dt), dq, dt, 0)
        for dq in range(nq)
        for dt in range(nt)
        if dq + dt
    ]
    cond_copy = remote(cond_ref, conds.at[c], cond_sems, (0,), 0, 0, 1)
    cond_copy.start()
    for copy in lat_copies:
        copy.start()
    leads = c == s

    def wqz_copy(k, dc):
        peer, core = flip(q, k), lax.rem(c + dc, nc)
        return pltpu.make_async_remote_copy(
            src_ref=wqkv_ref.at[peer * nc + core],
            dst_ref=wq.at[mine],
            send_sem=wqz_sems.at[0, k, dc],
            recv_sem=wqz_sems.at[1, k, 0],
            device_id={"queue": peer, "cfg": core},
            device_id_type=pl.DeviceIdType.MESH,
        )

    def wqy_copy(k, owner):
        slot = wq.at[flip(q, k) * nc + owner]
        return remote(slot, slot, wqy_sems, (k,), 0, 0, 0, 1)

    def piece_of(side, k):
        return wo.at[side, c, flip(q, k)]

    def woz_copy(k):
        return pltpu.make_async_remote_copy(
            src_ref=wout_ref,
            dst_ref=wo.at[t, c, q],
            send_sem=woz_sems.at[0, k],
            recv_sem=woz_sems.at[1, k],
            device_id={"queue": flip(q, k)},
            device_id_type=pl.DeviceIdType.MESH,
        )

    def woy_copy(k):
        return remote(piece_of(t, k), piece_of(t, k), woy_sems, (k,), 0, 0, 0, 1)

    def wox_copy(k):
        source = piece_of(t, k) if k else wout_ref
        return remote(source, piece_of(t, k), wox_sems, (k,), 0, 1, 0)

    def woc_copy(side, k):
        source = piece_of(t if side == 0 else 1 - t, k) if side or k else wout_ref
        target = piece_of(t if side == 0 else 1 - t, k)
        return remote(source, target, woc_sems, (side, k), 0, 0, 1)

    @pl.when(leads)
    def _():
        for k in reversed(range(1, nq)):
            for dc in range(nc):
                wqz_copy(k, dc).start()

    wq_partner = remote(wqkv_ref.at[q * nc + 1 - c], wq.at[mine], wq_sems, (0,), 0, 0, 1)
    wq_partner.start()
    wox_copy(0).start()
    woc_copy(0, 0).start()

    def arrive(dq):
        @pl.when(leads)
        def _():
            woz_copy(dq).wait_recv()
            woy_copy(dq).start()

        @pl.when(jnp.logical_not(leads))
        def _():
            woy_copy(dq).wait_recv()

        wox_copy(dq).start()
        woc_copy(0, dq).start()

    local_copies = [
        pltpu.make_async_copy(cells_ref, own_cells, local_sems.at[0]),
        pltpu.make_async_copy(cond_ref, conds.at[c], local_sems.at[1]),
        pltpu.make_async_copy(wqkv_ref.at[mine], wq.at[mine], local_sems.at[2]),
        pltpu.make_async_copy(wout_ref, wo.at[t, c, q], local_sems.at[3]),
    ]
    for copy in local_copies:
        copy.start()
    blank = jnp.zeros((window, head_dim, nt * LANES), f32)
    k_rows[:window] = blank
    v_rows[:window] = blank
    k_rows[total + window :] = blank
    v_rows[total + window :] = blank
    thin = jnp.zeros((window, 1, nt * LANES), f32)
    for ref in (key_scale, value_scale):
        ref[:window] = thin
        ref[total + window :] = thin
    for copy in local_copies:
        copy.wait()
    cond_copy.wait()
    for copy in lat_copies:
        copy.wait()

    extra = lax.broadcasted_iota(jnp.int32, (chans, LANES), 0)
    lane = lax.broadcasted_iota(jnp.int32, (chans, LANES), 1)
    first = (extra == 0) & (lane < tok_count)
    second = (extra == 1) & (lane >= tok_count) & (lane < 2 * tok_count)
    marks = jnp.where(first | second, 1.0, 0.0)

    def unpack(i, carry):
        for side in range(nt):
            block = got[side, i].astype(f32)
            for h in range(2):
                tokens = block[:, h * tok_count : (h + 1) * tok_count]
                spread = jnp.concatenate([tokens, tokens, jnp.zeros((chans, gap), f32)], axis=1)
                flag = block[:, 2 * tok_count + h : 2 * tok_count + h + 1]
                cells[side, 2 * i + h, :chans] = spread.astype(bf16)
                cells[side, 2 * i + h, chans:] = (marks + flag).astype(bf16)
        return carry

    lax.fori_loop(0, total // 2, unpack, 0)

    row_ids = lax.broadcasted_iota(jnp.int32, (rows, 1), 0)
    base[...] = jnp.zeros((rows, width), f32)
    base[:chans] = embed_ref[...].astype(f32)
    base[chans : chans + 1] = conds[0]
    base[chans + 1 : chans + 2] = conds[1]
    plain = base[...]
    centered = plain - jnp.mean(plain, axis=1, keepdims=True)
    gram = lax.dot_general(
        centered,
        centered,
        (((1,), (1,)), ((), ())),
        precision=HIGH,
        preferred_element_type=f32,
    ) * (1.0 / width)

    level_column = cells[0, :, row_level, :].astype(f32)
    level_ids = lax.broadcasted_iota(jnp.int32, (total, LANES), 1).astype(f32)
    one_hot = (level_column == level_ids).astype(f32)[:, :levels_all]
    shift = jnp.dot(one_hot, mod_ref[0], precision=HIGH, preferred_element_type=f32)
    scale = jnp.dot(one_hot, mod_ref[1], precision=HIGH, preferred_element_type=f32) + 1.0
    is_shift = (row_ids == chans + 2) | (row_ids == chans + 3)
    for f in range(total):
        block = jnp.where(is_shift, shift[f : f + 1], centered * scale[f : f + 1])
        high, low = split2(block)
        scaled_hi[f * rows : (f + 1) * rows] = high
        scaled_lo[f * rows : (f + 1) * rows] = low

    group = LANES // rows

    def frame_cells(f):
        return jnp.concatenate([cells[i, f].astype(f32) for i in range(nt)], axis=1)

    def prepare(f, carry):
        cell = jnp.where(row_ids < chans + 2, frame_cells(f), 0.0)
        spread = jnp.sum(
            cell * jnp.dot(gram, cell, precision=HIGH, preferred_element_type=f32),
            axis=0,
            keepdims=True,
        )
        spread = jnp.maximum(spread, 0.0) + EPS_NORM
        inverse = lax.rsqrt(spread)
        sigma = spread * inverse
        sigma_hi = sigma.astype(bf16).astype(f32)
        cell = jnp.where(row_ids == chans + 2, sigma_hi, cell)
        cell = jnp.where(row_ids == chans + 3, sigma - sigma_hi, cell)
        low_row = pl.multiple_of(lax.rem(f, group) * rows, rows)
        inputs[f, pl.ds(low_row, rows)] = cell.astype(bf16)
        inputs[f, pl.ds(low_row + LANES, rows)] = cell.astype(bf16)
        value_scale[f + window] = inverse
        return carry

    for step in range(nq):
        lax.fori_loop(step * frames, (step + 1) * frames, prepare, 0, unroll=4)
        k = nq - 1 - step
        if k:
            wqz_copy(k, 0).wait_recv()
            wqy_copy(k, s).start()

    @pl.when(leads)
    def _():
        for k in range(1, nq):
            woz_copy(k).start()

    wq_partner.wait()
    for dq in range(1, nq):
        wqy_copy(dq, 1 - s).wait_recv()
    weights = wq[...].reshape(width, wq.shape[2])
    proj[...] = jnp.dot(scaled_hi[...], weights, preferred_element_type=f32) + jnp.dot(
        scaled_lo[...], weights, preferred_element_type=f32
    )

    diagonal = lax.broadcasted_iota(jnp.int32, (head_dim, head_dim), 0) == (
        lax.broadcasted_iota(jnp.int32, (head_dim, head_dim), 1)
    )

    def column(gain_ref):
        return jnp.sum(jnp.where(diagonal, gain_ref[...], 0.0), axis=1, keepdims=True)

    gain = column(query_gain_ref) * column(key_gain_ref) * head_dim**-0.5
    for g in range(total // group):
        block = proj[g * LANES : (g + 1) * LANES].T
        high, low = split2(block)
        proj_t[g] = jnp.concatenate([high, low], axis=1)

    def project(f, carry):
        whole = jnp.dot(proj_t[f // group], inputs[f], preferred_element_type=f32)
        inverse = value_scale[f + window]
        query = whole[:head_dim]
        key = whole[head_dim : 2 * head_dim]

        def rms(part):
            spread = jnp.mean(part * part, axis=0, keepdims=True)
            return inverse * lax.rsqrt(spread * inverse * inverse + EPS_NORM)

        q_rows[f] = query * gain * rms(query)
        k_rows[f + window] = key
        key_scale[f + window] = rms(key)
        v_rows[f + window] = whole[2 * head_dim : 3 * head_dim]
        return carry

    for dq in range(1, nq):
        lax.fori_loop((dq - 1) * frames, dq * frames, project, 0, unroll=4)
        arrive(dq)
    lax.fori_loop((nq - 1) * frames, total, project, 0, unroll=4)

    own_lanes = 2 * tok_count
    rest_lanes = 2 * own_lanes - LANES
    tail = att_out.shape[2] - head_dim
    lane_ids = lax.broadcasted_iota(jnp.int32, (1, LANES), 1)
    own_lane = lane_ids < own_lanes
    rest_lane = lane_ids < rest_lanes

    def join(low, high):
        rest = pltpu.roll(high, own_lanes, 1)
        return jnp.concatenate([jnp.where(own_lane, low, rest), rest], axis=1)

    def attend(pair):
        done = []
        for inner in range(per_core):
            f = pair * per_core + inner
            cell = frame_cells(f)
            query = q_rows[f]
            numerator = jnp.zeros((head_dim, nt * LANES), f32)
            denominator = jnp.zeros((1, nt * LANES), f32)
            for o in range(span):
                score = jnp.sum(query * k_rows[f + o], axis=0, keepdims=True)
                row = row_level + 1 + o
                weight = jnp.exp(score * key_scale[f + o]) * cell[row : row + 1]
                numerator = numerator + (weight * value_scale[f + o]) * v_rows[f + o]
                denominator = denominator + weight
            done.append(numerator / denominator)
        for i in range(nt):
            low, high = (d[:, i * LANES : (i + 1) * LANES] for d in done)
            rest = pltpu.roll(high, own_lanes, 1)
            joined = jnp.where(own_lane, low, rest)
            upper = pltpu.roll(rest[head_dim - tail :], rest_lanes, 1)
            folded = jnp.where(rest_lane, rest[:tail], upper)
            att_out[pair, i] = jnp.concatenate([joined, folded], axis=0).astype(bf16)

    head = t * pairs + mine

    def att_copy(step, dt):
        pair = lax.rem(mine + step, pairs)
        other = lax.rem(t + dt, nt)
        return pltpu.make_async_remote_copy(
            src_ref=att_out.at[pair, other],
            dst_ref=att_in.at[head],
            send_sem=att_sems.at[0, step, dt],
            recv_sem=att_sems.at[1, step, dt],
            device_id={"queue": pair // nc, "tok": other, "cfg": lax.rem(pair, nc)},
            device_id_type=pl.DeviceIdType.MESH,
        )

    def attend_step(step, carry):
        attend(lax.rem(mine + step, pairs))
        for dt in range(nt):
            att_copy(step, dt).start()
        return carry

    lax.fori_loop(1, pairs, attend_step, 0)
    attend(mine)
    for dt in range(1, nt):
        att_copy(0, dt).start()
    att_in[head] = att_out[mine, t]

    own = join(*[cells[t, mine * per_core + i].astype(f32) for i in range(per_core)])
    embedded = dot00(plain, jnp.where(row_ids < chans + 2, own, 0.0), HIGH)
    own_level = own[row_level : row_level + 1]
    own_hot = (
        own_level == lax.broadcasted_iota(jnp.int32, (levels_all, 1), 0).astype(f32)
    ).astype(f32)
    gate = dot00(mod_ref[2], own_hot, HIGH)

    for dq in range(nq):
        wox_copy(dq).wait()
        woc_copy(1, dq).start()

    def att_wait(step, carry):
        for dt in range(nt):
            att_copy(step, dt).wait()
        return carry

    lax.fori_loop(1, pairs, att_wait, 0)
    for dt in range(1, nt):
        att_copy(0, dt).wait()
    for dq in range(nq):
        woc_copy(0, dq).wait()
        woc_copy(1, dq).wait()

    group = pairs * head_dim
    arrived = att_in[...].astype(f32)
    folded = arrived[:, head_dim:]
    upper = pltpu.roll(folded[:, 2 * tail - head_dim :], LANES - rest_lanes, 2)
    attended = jnp.concatenate(
        [arrived[:, :head_dim], jnp.concatenate([folded, upper], axis=1)], axis=2
    )
    attended = attended.reshape(nt * group, 2 * LANES).astype(bf16)
    slices = []
    for i in range(nt):
        by_core = [
            jnp.dot(
                wo[i, k].reshape(nq * wo.shape[3], group),
                attended[i * group : (i + 1) * group],
                preferred_element_type=f32,
            )
            for k in range(nc)
        ]
        slices.append(by_core)
    piece = wo.shape[3]
    mixed = jnp.concatenate(
        [
            sum(slices[i][k][j * piece : (j + 1) * piece] for i in range(nt))
            for j in range(nq)
            for k in range(nc)
        ],
        axis=0,
    )
    summed = embedded + gate * mixed
    deviate = summed - jnp.mean(summed, axis=0, keepdims=True)
    inverse = lax.rsqrt(jnp.mean(deviate * deviate, axis=0, keepdims=True) + EPS_NORM)
    rounded = deviate.astype(bf16)
    final_hi, final_lo = split2(wfinal_ref[...].astype(f32) * final_gain_ref[...])
    velocity = (
        jnp.dot(final_hi, rounded, preferred_element_type=f32)
        + jnp.dot(final_lo, rounded, preferred_element_type=f32)
    ) * inverse

    guidance = jnp.float32(0.0)
    for i in range(entries):
        guidance = guidance + jnp.where(index_ref[0] == i, table_ref[i], 0.0)

    def step_of(level):
        upcoming = noise_sigma(level / levels_all)
        current = noise_sigma((level + 1.0) / levels_all)
        return upcoming - current

    half = chans // nc
    for i in range(per_core):
        begin = i * own_lanes
        cond_vel = velocity[:, begin : begin + tok_count]
        uncond_vel = velocity[:, begin + tok_count : begin + 2 * tok_count]
        guided = uncond_vel + guidance * (cond_vel - uncond_vel)
        for k in range(nc):
            vel_half[k, i] = guided[k * half : (k + 1) * half]
        if i == 0:
            change = step_of(own_level[:, :tok_count])
            updated = latents_ref[0] + change * guided
            for k in range(nc):
                head_half[k] = updated[k * half : (k + 1) * half]

    own_slot = pl.ds(c * per_core, per_core)
    vel_copy = remote(vel_half.at[1 - c], vel_got, end_sems, (0,), 0, 0, 1)
    vel_copy.start()

    def head_copy(k):
        return pltpu.make_async_remote_copy(
            src_ref=head_half.at[k],
            dst_ref=head_got,
            send_sem=end_sems.at[0, 1 + k],
            recv_sem=end_sems.at[1, 1],
            device_id={"queue": lax.rem(q + nq - 1, nq), "cfg": k},
            device_id_type=pl.DeviceIdType.MESH,
        )

    @pl.when((c == 0) & (q > 0))
    def _():
        for k in range(nc):
            head_copy(k).start()

    guided_ref[own_slot] = vel_half[c]
    vel_copy.wait()
    guided_ref[pl.ds((1 - c) * per_core, per_core)] = vel_got[...]
    own_half = pl.ds(pl.multiple_of(c * half, half), half)
    for f in range(1, frames):
        level = cells[t, q * frames + f].astype(f32)[row_level : row_level + 1, :tok_count]
        queue_ref[f - 1] = latents_ref[f, own_half] + step_of(level) * guided_ref[f]

    @pl.when(q == nq - 1)
    def _():
        queue_ref[frames - 1] = noise_ref[...]

    @pl.when(q < nq - 1)
    def _():
        head_copy(0).wait_recv()
        queue_ref[frames - 1] = head_got[...]

    @pl.when((c == 0) & (q > 0))
    def _():
        for k in range(nc):
            head_copy(k).wait_send()

    for dq in range(1, nq):
        wqy_copy(dq, s).wait_send()

    @pl.when(leads)
    def _():
        for dq in range(1, nq):
            for dc in range(nc):
                wqz_copy(dq, dc).wait_send()
            woz_copy(dq).wait_send()
            woy_copy(dq).wait_send()


def on_device(
    latents,
    fresh_noise,
    levels,
    window_mask,
    cond_embed,
    level_mod,
    embed_weight,
    qkv_weight,
    query_gain,
    key_gain,
    out_weight,
    final_gain,
    final_weight,
    guide_table,
    guide_index,
):
    frames, chans, tok_count = latents.shape
    width = embed_weight.shape[1]
    head_dim = query_gain.shape[0]
    levels_all = level_mod.shape[0]
    nq, nt, nc = (lax.axis_size(a) for a in ("queue", "tok", "cfg"))
    shard_rows, _, local_cols = qkv_weight.shape
    pairs = nq * nc
    span = window_mask.shape[1]
    window = span // 2
    rows = 2 * chans
    fits = (
        local_cols == pairs * head_dim
        and frames % nc == 0
        and frames % 2 == 0
        and chans >= 5 + span
        and 2 * tok_count + 2 <= LANES
        and nc == 2
        and nt == 2
        and lax.axis_size("scene") == 2
        and chans % (8 * nc) == 0
        and 2 * tok_count <= LANES
        and levels_all <= LANES
        and nq == 4
        and frames == 2 * nc
        and 4 * tok_count == LANES + LANES // 2
        and frames == LANES // rows
    )
    if not fits:
        return on_device_plain(
            latents, fresh_noise, levels, window_mask, cond_embed, level_mod, embed_weight,
            qkv_weight, query_gain, key_gain, out_weight, final_gain, final_weight,
            guide_table, guide_index,
        )
    f32, bf16 = jnp.float32, jnp.bfloat16
    packed = -(-3 * head_dim // LANES) * LANES
    wqkv = qkv_weight.transpose(1, 0, 2)
    wout = out_weight.T
    wfinal = final_weight.T
    mods = level_mod.transpose(1, 0, 2)
    total = nq * frames
    per_core = frames // nc
    half = chans // nc
    tail = -(-head_dim // 16) * 8
    dims = (nq, nt, nc, frames, chans, head_dim, window, tok_count, guide_table.shape[0])
    vmem = pl.BlockSpec(memory_space=pltpu.VMEM)
    smem = pl.BlockSpec(memory_space=pltpu.SMEM)
    dma = pltpu.SemaphoreType.DMA
    out = jax.ShapeDtypeStruct((frames, half, tok_count), f32)
    staged = [
        cond_embed, mods, embed_weight, wqkv, query_gain[None], key_gain[None], wout,
        final_gain[None], wfinal, latents, fresh_noise,
    ]
    scalars = [guide_table, guide_index, levels, window_mask]
    anywhere = pl.BlockSpec(memory_space=pl.ANY)
    return pl.pallas_call(
        functools.partial(staged_kernel, dims, len(staged), len(scalars)),
        out_shape=(out, out),
        in_specs=[anywhere] * len(staged) + [smem] * len(scalars),
        out_specs=(vmem, vmem),
        scratch_shapes=[
            *[pltpu.VMEM(array.shape, array.dtype) for array in staged],
            dma((len(staged),)),
            pltpu.VMEM((frames // 2, chans, LANES), bf16),
            pltpu.VMEM((pairs, shard_rows, packed), bf16),
            pltpu.VMEM((nt, total // 2, chans, LANES), bf16),
            pltpu.VMEM((nt, total, rows, LANES), bf16),
            pltpu.VMEM((total, 2 * LANES, nt * LANES), bf16),
            pltpu.VMEM((total + 2 * window, 1, nt * LANES), f32),
            pltpu.VMEM((total + 2 * window, 1, nt * LANES), f32),
            pltpu.VMEM((total * rows // LANES, packed, 2 * LANES), bf16),
            pltpu.VMEM((nc, 1, width), f32),
            pltpu.VMEM((rows, width), f32),
            pltpu.VMEM((pairs, shard_rows, packed), bf16),
            pltpu.VMEM((nt, nc, nq, wout.shape[0], wout.shape[1]), bf16),
            pltpu.VMEM((total * rows, width), bf16),
            pltpu.VMEM((total * rows, width), bf16),
            pltpu.VMEM((total * rows, packed), f32),
            pltpu.VMEM((total, head_dim, nt * LANES), f32),
            pltpu.VMEM((total + 2 * window, head_dim, nt * LANES), f32),
            pltpu.VMEM((total + 2 * window, head_dim, nt * LANES), f32),
            pltpu.VMEM((pairs, nt, head_dim + tail, LANES), bf16),
            pltpu.VMEM((nt * pairs, head_dim + tail, LANES), bf16),
            pltpu.VMEM((nc, per_core, half, tok_count), f32),
            pltpu.VMEM((per_core, half, tok_count), f32),
            pltpu.VMEM((nc, half, tok_count), f32),
            pltpu.VMEM((half, tok_count), f32),
            dma((2, nq, nt)),
            dma((2, 1)),
            dma((2, 1)),
            dma((2, nq, nc)),
            dma((2, nq)),
            dma((2, nq)),
            dma((2, nq)),
            dma((2, nq)),
            dma((2, 2, nq)),
            dma((2, pairs, nt)),
            dma((2, 1 + nc)),
            dma((4,)),
        ],
        compiler_params=pltpu.CompilerParams(collective_id=0, has_side_effects=True),
    )(
        *staged, *scalars
    )


def solution(mesh):
    placed = (
        P(("scene", "queue"), None, "tok"),
        P(("scene", "cfg"), "tok"),
        P(("scene", "queue")),
        P(("scene", "queue"), None),
        P(("scene", "cfg"), None),
        P(),
        P(),
        P(("queue", "cfg"), None, "tok"),
        P(),
        P(),
        P("tok", ("queue", "cfg")),
        P(),
        P(),
        P(),
        P(),
    )
    return jax.shard_map(
        on_device,
        mesh=mesh,
        in_specs=placed,
        out_specs=(P(("scene", "queue"), "cfg", "tok"), P(("scene", "queue"), "cfg", "tok")),
        check_vma=False,
    )
```

```python
import functools

import jax
import jax.numpy as jnp
from jax import lax
from jax.experimental import pallas as pl
from jax.experimental.pallas import tpu as pltpu
from jax.sharding import PartitionSpec as P

LANES = 128
HIGH = lax.Precision.HIGHEST

EPS_NORM = 1e-06
TIME_SHIFT = 3.0


def with_halo(cells, sides, width):
    for axis, dim in sides:
        count = lax.axis_size(axis)
        ends = count - 1
        head = lax.slice_in_dim(cells, 0, width, axis=dim)
        tail = lax.slice_in_dim(cells, cells.shape[dim] - width, cells.shape[dim], axis=dim)
        cells = jnp.concatenate(
            [
                lax.ppermute(tail, axis, [(i, (i + 1) % count) for i in range(ends)]),
                cells,
                lax.ppermute(head, axis, [((i + 1) % count, i) for i in range(ends)]),
            ],
            axis=dim,
        )
    return cells


def from_partner(value, axis, bit):
    return lax.ppermute(value, axis, [(i, i ^ 1 << bit) for i in range(lax.axis_size(axis))])


def shifted(value, axis, steps):
    count = lax.axis_size(axis)
    initial, last = (max(0, -steps), min(count, count - steps))
    return lax.ppermute(value, axis, [(source, source + steps) for source in range(initial, last)])


def layer_norm(values):
    center = jnp.mean(values, axis=-1, keepdims=True)
    deviate = values - center
    spread = jnp.mean(deviate * deviate, axis=-1, keepdims=True)
    return deviate * lax.rsqrt(spread + EPS_NORM)


def rms_norm(values, scaling):
    return (
        values * lax.rsqrt(jnp.mean(values * values, axis=-1, keepdims=True) + EPS_NORM) * scaling
    )


def noise_sigma(fraction):
    return TIME_SHIFT * fraction / (1.0 + (TIME_SHIFT - 1.0) * fraction)


def temporal_attention(
    queries, key_rows, value_rows, window_mask, first_frame, total_frames, window
):
    frames = queries.shape[0]
    numerator = jnp.zeros(queries.shape, jnp.float32)
    denominator = jnp.zeros(queries.shape[:-1], jnp.float32)
    for offset in range(2 * window + 1):
        near_keys = key_rows[offset : offset + frames].astype(jnp.float32)
        near_values = value_rows[offset : offset + frames].astype(jnp.float32)
        scores = jnp.sum(queries * near_keys, axis=-1) * queries.shape[-1] ** (-0.5)
        target = first_frame + jnp.arange(frames, dtype=jnp.int32) + (offset - window)
        allowed = (window_mask[:, offset] == 1) & (target >= 0) & (target < total_frames)
        weights = jnp.exp(scores) * allowed.astype(jnp.float32)[:, None, None]
        numerator = numerator + weights[..., None] * near_values
        denominator = denominator + weights
    return numerator / denominator[..., None]


def on_device_plain(
    latents,
    fresh_noise,
    levels,
    window_mask,
    cond_embed,
    level_mod,
    embed_weight,
    qkv_weight,
    query_gain,
    key_gain,
    out_weight,
    final_gain,
    final_weight,
    guide_table,
    guide_index,
):
    frames = latents.shape[0]
    tok_count = latents.shape[2]
    model_width = embed_weight.shape[1]
    head_dim = query_gain.shape[0]
    levels_all = level_mod.shape[0]
    queue_count = lax.axis_size("queue")
    all_tokens = lax.all_gather(latents, "tok", axis=2, tiled=True)
    seq_tokens = all_tokens.shape[2]
    row_count = frames * seq_tokens
    embedded = (
        jnp.einsum(
            "fcs,cd->fsd",
            all_tokens.astype(jnp.bfloat16),
            embed_weight,
            preferred_element_type=jnp.float32,
        )
        + cond_embed[0]
    )
    one_hot = (levels[:, None] == jnp.arange(levels_all, dtype=jnp.int32)[None, :]).astype(
        jnp.float32
    )
    modulate = jnp.dot(
        one_hot, level_mod.reshape(levels_all, 3 * model_width), precision=lax.Precision.HIGHEST
    ).reshape(frames, 3, model_width)
    normed = (layer_norm(embedded) * (1.0 + modulate[:, None, 1]) + modulate[:, None, 0]).astype(
        jnp.bfloat16
    )
    norm_rows = normed.reshape(row_count, model_width)
    local_cols = qkv_weight.shape[2]
    shard_piece = lax.all_gather(qkv_weight, ("queue", "cfg"), axis=0, tiled=True)
    flat_piece = shard_piece.reshape(shard_piece.shape[0], 3 * local_cols)
    projected = jnp.dot(norm_rows, flat_piece, preferred_element_type=jnp.float32)
    projected = projected.reshape(frames, seq_tokens, 3, local_cols // head_dim, head_dim)
    queries = rms_norm(projected[:, :, 0], query_gain)
    keys_values = jnp.stack(
        [
            rms_norm(projected[:, :, 1], key_gain).astype(jnp.bfloat16),
            projected[:, :, 2].astype(jnp.bfloat16),
        ]
    )
    widened = with_halo(keys_values, (("queue", 1),), frames)
    first_frame = lax.axis_index("queue") * frames
    attended = temporal_attention(
        queries, widened[0], widened[1], window_mask, first_frame, frames * queue_count, frames
    )
    attended = attended.astype(jnp.bfloat16).reshape(frames, seq_tokens, local_cols)
    flat_heads = attended.reshape(row_count, local_cols)
    partial_value = jnp.dot(
        flat_heads,
        lax.all_gather(out_weight, ("queue", "cfg"), axis=1, tiled=True),
        preferred_element_type=jnp.float32,
    )
    mixed_out = lax.psum_scatter(
        partial_value.reshape(frames, seq_tokens, model_width).astype(jnp.bfloat16),
        "tok",
        scatter_dimension=1,
        tiled=True,
    ).astype(jnp.float32)
    own_start = lax.axis_index("tok") * tok_count
    own_embed = lax.dynamic_slice_in_dim(embedded, own_start, tok_count, 1)
    summed = own_embed + modulate[:, None, 2] * mixed_out
    final_rows = (layer_norm(summed) * final_gain).astype(jnp.bfloat16)
    velocity = jnp.einsum(
        "ftd,dc->fct", final_rows, final_weight, preferred_element_type=jnp.float32
    )
    half_values = velocity.shape[1] // 2
    branch_index = lax.axis_index("cfg")
    own_first = branch_index * half_values
    other_first = (1 - branch_index) * half_values
    outgoing = lax.dynamic_slice_in_dim(velocity, other_first, half_values, 1)
    partner = from_partner(outgoing, "cfg", 0)
    mine = lax.dynamic_slice_in_dim(velocity, own_first, half_values, 1)
    is_cond = branch_index == 0
    cond_vel = jnp.where(is_cond, mine, partner)
    uncond_vel = jnp.where(is_cond, partner, mine)
    entries = guide_table.shape[0]
    guidance = jnp.sum(
        guide_table * (jnp.arange(entries, dtype=jnp.int32) == guide_index[0]).astype(jnp.float32)
    )
    guided = uncond_vel + guidance * (cond_vel - uncond_vel)
    current = noise_sigma((levels + 1).astype(jnp.float32) / levels_all)
    upcoming = noise_sigma(levels.astype(jnp.float32) / levels_all)
    own_latents = lax.dynamic_slice_in_dim(latents, own_first, half_values, 1)
    updated = own_latents + (upcoming - current)[:, None, None] * guided
    incoming = shifted(updated[:1], "queue", -1)
    is_last = lax.axis_index("queue") == queue_count - 1
    incoming = jnp.where(is_last, fresh_noise[None], incoming)
    new_queue = jnp.concatenate([updated[1:], incoming], axis=0)
    return (guided, new_queue)


def flip(index, mask):
    result, bit = index, 1
    while bit <= mask:
        if mask & bit:
            result = result + bit - 2 * bit * lax.rem(index // bit, 2)
        bit *= 2
    return result


def split2(value):
    high = value.astype(jnp.bfloat16)
    return high, (value - high.astype(jnp.float32)).astype(jnp.bfloat16)


def dot00(left, right, precision=None):
    return lax.dot_general(
        left,
        right,
        (((0,), (0,)), ((), ())),
        precision=precision,
        preferred_element_type=jnp.float32,
    )


def staged_kernel(dims, staged, plain, *refs):
    sources, rest = refs[:staged], refs[staged:]
    others, scratch = rest[: plain + 2], rest[plain + 2 :]
    holders, sems = scratch[:staged], scratch[staged]
    loads = [
        pltpu.make_async_copy(sources[i], holders[i], sems.at[i]) for i in range(staged)
    ]
    for load in loads:
        load.start()
    fused_kernel(dims, loads, *holders, *others, *scratch[staged + 1 :])


def fused_kernel(
    dims,
    loads,
    cond_ref,
    mod_ref,
    embed_ref,
    qkv_ref,
    query_gain_ref,
    key_gain_ref,
    wout_ref,
    final_gain_ref,
    wfinal_ref,
    latents_ref,
    noise_ref,
    table_ref,
    index_ref,
    levels_ref,
    mask_ref,
    guided_ref,
    queue_ref,
    cells_ref,
    wqkv_ref,
    got,
    cells,
    inputs,
    key_scale,
    value_scale,
    proj_t,
    embed_rows,
    gate_rows,
    conds,
    base,
    wq,
    wo,
    scaled_hi,
    scaled_lo,
    proj,
    q_rows,
    k_rows,
    v_rows,
    att_out,
    att_in,
    vel_half,
    vel_got,
    head_half,
    head_got,
    lat_sems,
    cond_sems,
    wq_sems,
    wqz_sems,
    wqy_sems,
    woz_sems,
    woy_sems,
    wox_sems,
    woc_sems,
    att_sems,
    end_sems,
    local_sems,
):
    nq, nt, nc, frames, chans, head_dim, window, tok_count, entries = dims
    span = 2 * window + 1
    total = nq * frames
    per_core = frames // nc
    pairs = nq * nc
    levels_all = mod_ref.shape[1]
    width = embed_ref.shape[1]
    row_level = chans + 4
    rows = cells.shape[2]
    f32, bf16 = jnp.float32, jnp.bfloat16

    s = lax.axis_index("scene")
    q = lax.axis_index("queue")
    t = lax.axis_index("tok")
    c = lax.axis_index("cfg")
    mine = q * nc + c

    barrier = pltpu.get_barrier_semaphore()
    peers = 0
    for dq in range(nq):
        for dt in range(nt):
            for dc in range(nc):
                if dq + dt + dc:
                    peers += 1
                    pl.semaphore_signal(
                        barrier,
                        inc=1,
                        device_id={
                            "queue": lax.rem(q + dq, nq),
                            "tok": lax.rem(t + dt, nt),
                            "cfg": lax.rem(c + dc, nc),
                        },
                        device_id_type=pl.DeviceIdType.MESH,
                    )
    pl.semaphore_signal(
        barrier,
        inc=1,
        device_id={"scene": 1 - s},
        device_id_type=pl.DeviceIdType.MESH,
    )
    for load in loads:
        load.wait()
    gap = LANES - 2 * tok_count
    flag_row = lax.broadcasted_iota(jnp.int32, (chans, gap), 0)
    flag_lane = lax.broadcasted_iota(jnp.int32, (chans, gap), 1)
    for i in range(frames // 2):
        flags = jnp.zeros((chans, gap), f32)
        for h in range(2):
            f = 2 * i + h
            flags = jnp.where(
                (flag_lane == h) & (flag_row == 4), levels_ref[f].astype(f32), flags
            )
            for o in range(span):
                flags = jnp.where(
                    (flag_lane == h) & (flag_row == 5 + o), mask_ref[f, o].astype(f32), flags
                )
        cells_ref[i] = jnp.concatenate(
            [latents_ref[2 * i], latents_ref[2 * i + 1], flags], axis=1
        ).astype(bf16)
    packed = wqkv_ref.shape[2]
    empty = jnp.zeros((qkv_ref.shape[1], packed - 3 * head_dim), f32)
    thirds = [qkv_ref[i].astype(f32) for i in range(3)]
    for j in range(pairs):
        cut = [part[:, j * head_dim : (j + 1) * head_dim] for part in thirds]
        wqkv_ref[j] = jnp.concatenate([*cut, empty], axis=1).astype(bf16)
    inputs[...] = jnp.zeros(inputs.shape, bf16)
    pl.semaphore_wait(barrier, peers + 1)

    def remote(source, target, sems, place, dq, dt, dc, ds=0):
        return pltpu.make_async_remote_copy(
            src_ref=source,
            dst_ref=target,
            send_sem=sems.at[(0, *place)],
            recv_sem=sems.at[(1, *place)],
            device_id={
                "scene": lax.rem(s + ds, 2),
                "queue": lax.rem(q + dq, nq),
                "tok": lax.rem(t + dt, nt),
                "cfg": lax.rem(c + dc, nc),
            },
            device_id_type=pl.DeviceIdType.MESH,
        )

    lat_copies = [
        remote(cells_ref.at[c], got.at[c, t, q], lat_sems, (dq, dt), dq, dt, 0)
        for dq in range(nq)
        for dt in range(nt)
        if dq + dt
    ]
    lat_forward = remote(got.at[c], got.at[c], lat_sems, (0, 0), 0, 0, 1)
    cond_copy = remote(cond_ref, conds.at[c], cond_sems, (0,), 0, 0, 1)
    cond_copy.start()
    for copy in lat_copies:
        copy.start()
    leads = c == s
    near = flip(q, 1)

    def wqz_copy(k, dc):
        peer, core = flip(q, k), lax.rem(c + dc, nc)
        return pltpu.make_async_remote_copy(
            src_ref=wqkv_ref.at[peer * nc + core],
            dst_ref=wq.at[mine],
            send_sem=wqz_sems.at[0, k, dc],
            recv_sem=wqz_sems.at[1, k, c if k == 1 else 0],
            device_id={"queue": peer, "cfg": core},
            device_id_type=pl.DeviceIdType.MESH,
        )

    def near_copy(owner):
        slot = wq.at[near * nc + owner]
        return pltpu.make_async_remote_copy(
            src_ref=slot,
            dst_ref=slot,
            send_sem=wqz_sems.at[0, 0, owner],
            recv_sem=wqz_sems.at[1, 1, owner],
            device_id={"queue": near},
            device_id_type=pl.DeviceIdType.MESH,
        )

    def wqy_copy(k, owner):
        slot = wq.at[flip(q, k) * nc + owner]
        return remote(slot, slot, wqy_sems, (k,), 0, 0, 0, 1)

    places = tuple(flip(q, p) for p in range(nq))
    pieces = len(places)
    shared = (2, 3)

    def piece_of(side, p):
        return wo.at[t if side == 0 else 1 - t, c, places[p]]

    def woz_copy(p):
        return pltpu.make_async_remote_copy(
            src_ref=wout_ref,
            dst_ref=wo.at[t, c, q],
            send_sem=woz_sems.at[0, p],
            recv_sem=woz_sems.at[1, p],
            device_id={"queue": places[p]},
            device_id_type=pl.DeviceIdType.MESH,
        )

    def woy_copy(side, p):
        return remote(piece_of(side, p), piece_of(side, p), woy_sems, (side, p), 0, 0, 0, 1)

    def wox_copy(p):
        return remote(piece_of(0, p) if p else wout_ref, piece_of(0, p), wox_sems, (p,), 0, 1, 0)

    def woc_copy(side, p):
        source = piece_of(side, p) if side or p else wout_ref
        return remote(source, piece_of(side, p), woc_sems, (side, p), 0, 0, 1)

    def arrive(p):
        @pl.when(leads)
        def _():
            woz_copy(p).wait_recv()
            if p in shared:
                wox_copy(p).start()
            woy_copy(0, p).start()

        @pl.when(jnp.logical_not(leads))
        def _():
            woy_copy(0, p).wait_recv()

        if p not in shared:
            wox_copy(p).start()
        woc_copy(0, p).start()

    def arrive_x(p):
        if p in shared:
            @pl.when(leads)
            def _():
                wox_copy(p).wait_recv()
                woy_copy(1, p).start()

            @pl.when(jnp.logical_not(leads))
            def _():
                woy_copy(1, p).wait_recv()
        else:
            wox_copy(p).wait_recv()
        woc_copy(1, p).start()

    @pl.when(leads)
    def _():
        for dc in range(nc):
            wqz_copy(3, dc).start()

    @pl.when(leads)
    def _():
        for dc in range(nc):
            wqz_copy(1, dc).start()

    wq_partner = remote(wqkv_ref.at[q * nc + 1 - c], wq.at[mine], wq_sems, (0,), 0, 0, 1)
    wq_partner.start()
    wox_copy(0).start()
    woc_copy(0, 0).start()

    local_copies = [
        pltpu.make_async_copy(cells_ref.at[c], got.at[c, t, q], local_sems.at[0]),
        pltpu.make_async_copy(cond_ref, conds.at[c], local_sems.at[1]),
        pltpu.make_async_copy(wqkv_ref.at[mine], wq.at[mine], local_sems.at[2]),
        pltpu.make_async_copy(wout_ref, wo.at[t, c, q], local_sems.at[3]),
    ]
    for copy in local_copies:
        copy.start()
    blank = jnp.zeros((window, head_dim, nt * LANES), f32)
    k_rows[:window] = blank
    v_rows[:window] = blank
    k_rows[total + window :] = blank
    v_rows[total + window :] = blank
    thin = jnp.zeros((window, 1, nt * LANES), f32)
    for ref in (key_scale, value_scale):
        ref[:window] = thin
        ref[total + window :] = thin
    for copy in local_copies:
        copy.wait()
    cond_copy.wait()
    row_ids = lax.broadcasted_iota(jnp.int32, (rows, 1), 0)
    base[...] = jnp.zeros((rows, width), f32)
    base[:chans] = embed_ref[...].astype(f32)
    base[chans : chans + 1] = conds[0]
    base[chans + 1 : chans + 2] = conds[1]
    plain = base[...]
    centered = plain - jnp.mean(plain, axis=1, keepdims=True)
    gram = lax.dot_general(
        centered,
        centered,
        (((1,), (1,)), ((), ())),
        precision=HIGH,
        preferred_element_type=f32,
    ) * (1.0 / width)

    @pl.when(leads)
    def _():
        for k in (3, 1):
            for dc in range(nc):
                wqz_copy(k, dc).wait_send()
        for dc in range(nc):
            wqz_copy(2, dc).start()

    @pl.when(jnp.logical_not(leads))
    def _():
        for dc in range(nc):
            wqz_copy(1, dc).start()

    wqz_copy(3, 0).wait_recv()
    wqy_copy(3, s).start()
    for copy in lat_copies:
        copy.wait()
    lat_forward.start()
    lat_forward.wait()

    extra = lax.broadcasted_iota(jnp.int32, (chans, LANES), 0)
    lane = lax.broadcasted_iota(jnp.int32, (chans, LANES), 1)
    first = (extra == 0) & (lane < tok_count)
    second = (extra == 1) & (lane >= tok_count) & (lane < 2 * tok_count)
    marks = jnp.where(first | second, 1.0, 0.0)

    def unpack(i, carry):
        for side in range(nt):
            block = got[lax.rem(i, nc), side, i // nc].astype(f32)
            for h in range(2):
                tokens = block[:, h * tok_count : (h + 1) * tok_count]
                spread = jnp.concatenate([tokens, tokens, jnp.zeros((chans, gap), f32)], axis=1)
                flag = block[:, 2 * tok_count + h : 2 * tok_count + h + 1]
                cells[side, 2 * i + h, :chans] = spread.astype(bf16)
                cells[side, 2 * i + h, chans:] = (marks + flag).astype(bf16)
        return carry

    lax.fori_loop(0, total // 2, unpack, 0)

    level_column = cells[0, :, row_level, :].astype(f32)
    level_ids = lax.broadcasted_iota(jnp.int32, (total, LANES), 1).astype(f32)
    one_hot = (level_column == level_ids).astype(f32)[:, :levels_all]
    shift = jnp.dot(one_hot, mod_ref[0], precision=HIGH, preferred_element_type=f32)
    scale = jnp.dot(one_hot, mod_ref[1], precision=HIGH, preferred_element_type=f32) + 1.0
    is_shift = (row_ids == chans + 2) | (row_ids == chans + 3)
    for f in range(total):
        block = jnp.where(is_shift, shift[f : f + 1], centered * scale[f : f + 1])
        high, low = split2(block)
        scaled_hi[f * rows : (f + 1) * rows] = high
        scaled_lo[f * rows : (f + 1) * rows] = low

    group = LANES // rows

    def frame_cells(f):
        return jnp.concatenate([cells[i, f].astype(f32) for i in range(nt)], axis=1)

    def prepare(f, carry):
        cell = jnp.where(row_ids < chans + 2, frame_cells(f), 0.0)
        spread = jnp.sum(
            cell * jnp.dot(gram, cell, precision=HIGH, preferred_element_type=f32),
            axis=0,
            keepdims=True,
        )
        spread = jnp.maximum(spread, 0.0) + EPS_NORM
        inverse = lax.rsqrt(spread)
        sigma = spread * inverse
        sigma_hi = sigma.astype(bf16).astype(f32)
        cell = jnp.where(row_ids == chans + 2, sigma_hi, cell)
        cell = jnp.where(row_ids == chans + 3, sigma - sigma_hi, cell)
        low_row = pl.multiple_of(lax.rem(f, group) * rows, rows)
        inputs[f, pl.ds(low_row, rows)] = cell.astype(bf16)
        inputs[f, pl.ds(low_row + LANES, rows)] = cell.astype(bf16)
        value_scale[f + window] = inverse
        return carry

    lax.fori_loop(0, total // 2, prepare, 0, unroll=4)
    @pl.when(leads)
    def _():
        woz_copy(1).start()

    lax.fori_loop(total // 2, total, prepare, 0, unroll=4)
    arrive_x(0)
    wqz_copy(2, 0).wait_recv()
    wqy_copy(2, s).start()

    @pl.when(leads)
    def _():
        for p in range(2, pieces):
            woz_copy(p).start()

    arrive(1)
    own_lanes = 2 * tok_count
    rest_lanes = 2 * own_lanes - LANES
    tail = att_out.shape[2] - head_dim
    lane_ids = lax.broadcasted_iota(jnp.int32, (1, LANES), 1)
    own_lane = lane_ids < own_lanes
    rest_lane = lane_ids < rest_lanes

    def join(low, high):
        rest = pltpu.roll(high, own_lanes, 1)
        return jnp.concatenate([jnp.where(own_lane, low, rest), rest], axis=1)

    own = join(*[cells[t, mine * per_core + i].astype(f32) for i in range(per_core)])
    embed_rows[...] = dot00(plain, jnp.where(row_ids < chans + 2, own, 0.0), HIGH)
    own_level = own[row_level : row_level + 1]
    own_hot = (
        own_level == lax.broadcasted_iota(jnp.int32, (levels_all, 1), 0).astype(f32)
    ).astype(f32)
    gate_rows[...] = dot00(mod_ref[2], own_hot, HIGH)

    wq_partner.wait()
    for k in (3, 2):
        wqy_copy(k, 1 - s).wait_recv()
    near_copy(0).wait_recv()
    near_copy(1).wait_recv()
    weights = wq[...].reshape(width, wq.shape[2])
    proj[...] = jnp.dot(scaled_hi[...], weights, preferred_element_type=f32) + jnp.dot(
        scaled_lo[...], weights, preferred_element_type=f32
    )

    diagonal = lax.broadcasted_iota(jnp.int32, (head_dim, head_dim), 0) == (
        lax.broadcasted_iota(jnp.int32, (head_dim, head_dim), 1)
    )

    def column(gain_ref):
        return jnp.sum(jnp.where(diagonal, gain_ref[...], 0.0), axis=1, keepdims=True)

    gain = column(query_gain_ref) * column(key_gain_ref) * head_dim**-0.5
    for g in range(total // group):
        block = proj[g * LANES : (g + 1) * LANES].T
        high, low = split2(block)
        proj_t[g] = jnp.concatenate([high, low], axis=1)

    def project(f, carry):
        whole = jnp.dot(proj_t[f // group], inputs[f], preferred_element_type=f32)
        inverse = value_scale[f + window]
        query = whole[:head_dim]
        key = whole[head_dim : 2 * head_dim]

        def rms(part):
            spread = jnp.mean(part * part, axis=0, keepdims=True)
            return inverse * lax.rsqrt(spread * inverse * inverse + EPS_NORM)

        q_rows[f] = query * gain * rms(query)
        k_rows[f + window] = key
        key_scale[f + window] = rms(key)
        v_rows[f + window] = whole[2 * head_dim : 3 * head_dim]
        return carry

    lax.fori_loop(0, total // 2, project, 0, unroll=4)
    arrive(2)
    lax.fori_loop(total // 2, total, project, 0, unroll=4)
    arrive_x(1)
    arrive(3)
    def attend(pair):
        done = []
        for inner in range(per_core):
            f = pair * per_core + inner
            cell = frame_cells(f)
            query = q_rows[f]
            numerator = jnp.zeros((head_dim, nt * LANES), f32)
            denominator = jnp.zeros((1, nt * LANES), f32)
            for o in range(span):
                score = jnp.sum(query * k_rows[f + o], axis=0, keepdims=True)
                row = row_level + 1 + o
                weight = jnp.exp(score * key_scale[f + o]) * cell[row : row + 1]
                numerator = numerator + (weight * value_scale[f + o]) * v_rows[f + o]
                denominator = denominator + weight
            done.append(numerator / denominator)
        for i in range(nt):
            low, high = (d[:, i * LANES : (i + 1) * LANES] for d in done)
            rest = pltpu.roll(high, own_lanes, 1)
            joined = jnp.where(own_lane, low, rest)
            upper = pltpu.roll(rest[head_dim - tail :], rest_lanes, 1)
            folded = jnp.where(rest_lane, rest[:tail], upper)
            att_out[pair, i] = jnp.concatenate([joined, folded], axis=0).astype(bf16)

    head = t * pairs + mine

    def att_copy(step, dt):
        pair = lax.rem(mine + step, pairs)
        other = lax.rem(t + dt, nt)
        return pltpu.make_async_remote_copy(
            src_ref=att_out.at[pair, other],
            dst_ref=att_in.at[head],
            send_sem=att_sems.at[0, step, dt],
            recv_sem=att_sems.at[1, step, dt],
            device_id={"queue": pair // nc, "tok": other, "cfg": lax.rem(pair, nc)},
            device_id_type=pl.DeviceIdType.MESH,
        )

    def attend_step(step, carry):
        attend(lax.rem(mine + step, pairs))
        for dt in range(nt):
            att_copy(step, dt).start()
        return carry

    lax.fori_loop(1, pairs, attend_step, 0)
    attend(mine)
    for dt in range(1, nt):
        att_copy(0, dt).start()
    att_in[head] = att_out[mine, t]

    arrive_x(2)
    arrive_x(3)

    def att_wait(step, carry):
        for dt in range(nt):
            att_copy(step, dt).wait()
        return carry

    lax.fori_loop(1, pairs, att_wait, 0)
    for dt in range(1, nt):
        att_copy(0, dt).wait()
    for p in range(pieces):
        woc_copy(0, p).wait()
        woc_copy(1, p).wait()
    for p in range(pieces):
        if p not in shared:
            wox_copy(p).wait_send()

    group = pairs * head_dim
    arrived = att_in[...].astype(f32)
    folded = arrived[:, head_dim:]
    upper = pltpu.roll(folded[:, 2 * tail - head_dim :], LANES - rest_lanes, 2)
    attended = jnp.concatenate(
        [arrived[:, :head_dim], jnp.concatenate([folded, upper], axis=1)], axis=2
    )
    attended = attended.reshape(nt * group, 2 * LANES).astype(bf16)
    slices = []
    for i in range(nt):
        by_core = [
            jnp.dot(
                wo[i, k].reshape(nq * wo.shape[3], group),
                attended[i * group : (i + 1) * group],
                preferred_element_type=f32,
            )
            for k in range(nc)
        ]
        slices.append(by_core)
    piece = wo.shape[3]
    mixed = jnp.concatenate(
        [
            sum(slices[i][k][j * piece : (j + 1) * piece] for i in range(nt))
            for j in range(nq)
            for k in range(nc)
        ],
        axis=0,
    )
    summed = embed_rows[...] + gate_rows[...] * mixed
    deviate = summed - jnp.mean(summed, axis=0, keepdims=True)
    inverse = lax.rsqrt(jnp.mean(deviate * deviate, axis=0, keepdims=True) + EPS_NORM)
    rounded = deviate.astype(bf16)
    final_hi, final_lo = split2(
        wfinal_ref[...].astype(f32)
        * jnp.concatenate([final_gain_ref[i : i + 1] for i in range(width // LANES)], axis=1)
    )
    velocity = (
        jnp.dot(final_hi, rounded, preferred_element_type=f32)
        + jnp.dot(final_lo, rounded, preferred_element_type=f32)
    ) * inverse

    guidance = jnp.float32(0.0)
    for i in range(entries):
        guidance = guidance + jnp.where(index_ref[0] == i, table_ref[i], 0.0)

    def step_of(level):
        upcoming = noise_sigma(level / levels_all)
        current = noise_sigma((level + 1.0) / levels_all)
        return upcoming - current

    half = chans // nc
    for i in range(per_core):
        begin = i * own_lanes
        cond_vel = velocity[:, begin : begin + tok_count]
        uncond_vel = velocity[:, begin + tok_count : begin + 2 * tok_count]
        guided = uncond_vel + guidance * (cond_vel - uncond_vel)
        for k in range(nc):
            vel_half[k, i] = guided[k * half : (k + 1) * half]
        if i == 0:
            change = step_of(own_level[:, :tok_count])
            updated = latents_ref[0] + change * guided
            for k in range(nc):
                head_half[k] = updated[k * half : (k + 1) * half]

    own_slot = pl.ds(c * per_core, per_core)
    vel_copy = remote(vel_half.at[1 - c], vel_got, end_sems, (0,), 0, 0, 1)
    vel_copy.start()

    def head_copy(k):
        return pltpu.make_async_remote_copy(
            src_ref=head_half.at[k],
            dst_ref=head_got,
            send_sem=end_sems.at[0, 1 + k],
            recv_sem=end_sems.at[1, 1],
            device_id={"queue": lax.rem(q + nq - 1, nq), "cfg": k},
            device_id_type=pl.DeviceIdType.MESH,
        )

    @pl.when((c == 0) & (q > 0))
    def _():
        for k in range(nc):
            head_copy(k).start()

    guided_ref[own_slot] = vel_half[c]
    vel_copy.wait()
    guided_ref[pl.ds((1 - c) * per_core, per_core)] = vel_got[...]
    own_half = pl.ds(pl.multiple_of(c * half, half), half)
    for f in range(1, frames):
        level = cells[t, q * frames + f].astype(f32)[row_level : row_level + 1, :tok_count]
        queue_ref[f - 1] = latents_ref[f, own_half] + step_of(level) * guided_ref[f]

    @pl.when(q == nq - 1)
    def _():
        queue_ref[frames - 1] = noise_ref[...]

    @pl.when(q < nq - 1)
    def _():
        head_copy(0).wait_recv()
        queue_ref[frames - 1] = head_got[...]

    @pl.when((c == 0) & (q > 0))
    def _():
        for k in range(nc):
            head_copy(k).wait_send()

    for k in (3, 2):
        wqy_copy(k, s).wait_send()

    @pl.when(jnp.logical_not(leads))
    def _():
        for dc in range(nc):
            wqz_copy(1, dc).wait_send()

    @pl.when(leads)
    def _():
        for dc in range(nc):
            wqz_copy(2, dc).wait_send()
        for p in range(1, pieces):
            woz_copy(p).wait_send()
            woy_copy(0, p).wait_send()
            if p in shared:
                wox_copy(p).wait_send()
                woy_copy(1, p).wait_send()


def hand_on(guided_ref, queue_ref, guided_out, queue_out):
    guided_out[...] = guided_ref[...]
    queue_out[...] = queue_ref[...]


def on_device(
    latents,
    fresh_noise,
    levels,
    window_mask,
    cond_embed,
    level_mod,
    embed_weight,
    qkv_weight,
    query_gain,
    key_gain,
    out_weight,
    final_gain,
    final_weight,
    guide_table,
    guide_index,
):
    frames, chans, tok_count = latents.shape
    width = embed_weight.shape[1]
    head_dim = query_gain.shape[0]
    levels_all = level_mod.shape[0]
    nq, nt, nc = (lax.axis_size(a) for a in ("queue", "tok", "cfg"))
    shard_rows, _, local_cols = qkv_weight.shape
    pairs = nq * nc
    span = window_mask.shape[1]
    window = span // 2
    rows = 2 * chans
    fits = (
        local_cols == pairs * head_dim
        and frames % nc == 0
        and frames % 2 == 0
        and chans >= 5 + span
        and 2 * tok_count + 2 <= LANES
        and nc == 2
        and nt == 2
        and lax.axis_size("scene") == 2
        and chans % (8 * nc) == 0
        and 2 * tok_count <= LANES
        and levels_all <= LANES
        and nq == 4
        and width % LANES == 0
        and frames == 2 * nc
        and 4 * tok_count == LANES + LANES // 2
        and frames == LANES // rows
    )
    if not fits:
        return on_device_plain(
            latents, fresh_noise, levels, window_mask, cond_embed, level_mod, embed_weight,
            qkv_weight, query_gain, key_gain, out_weight, final_gain, final_weight,
            guide_table, guide_index,
        )
    f32, bf16 = jnp.float32, jnp.bfloat16
    packed = -(-3 * head_dim // LANES) * LANES
    wqkv = qkv_weight.transpose(1, 0, 2)
    wout = out_weight.T
    wfinal = final_weight.T
    mods = level_mod.transpose(1, 0, 2)
    total = nq * frames
    per_core = frames // nc
    half = chans // nc
    tail = -(-head_dim // 16) * 8
    dims = (nq, nt, nc, frames, chans, head_dim, window, tok_count, guide_table.shape[0])
    vmem = pl.BlockSpec(memory_space=pltpu.VMEM)
    smem = pl.BlockSpec(memory_space=pltpu.SMEM)
    dma = pltpu.SemaphoreType.DMA
    out = jax.ShapeDtypeStruct((frames, half, tok_count), f32)
    staged = [
        cond_embed, mods, embed_weight, wqkv, query_gain[None], key_gain[None], wout,
        final_gain.reshape(width // LANES, LANES), wfinal, latents, fresh_noise,
    ]
    scalars = [guide_table, guide_index, levels, window_mask]
    anywhere = pl.BlockSpec(memory_space=pl.ANY)
    results = pl.pallas_call(
        functools.partial(staged_kernel, dims, len(staged), len(scalars)),
        out_shape=(out, out),
        in_specs=[anywhere] * len(staged) + [smem] * len(scalars),
        out_specs=(vmem, vmem),
        scratch_shapes=[
            *[pltpu.VMEM(array.shape, array.dtype) for array in staged],
            dma((len(staged),)),
            pltpu.VMEM((frames // 2, chans, LANES), bf16),
            pltpu.VMEM((pairs, shard_rows, packed), bf16),
            pltpu.VMEM((nc, nt, nq, chans, LANES), bf16),
            pltpu.VMEM((nt, total, rows, LANES), bf16),
            pltpu.VMEM((total, 2 * LANES, nt * LANES), bf16),
            pltpu.VMEM((total + 2 * window, 1, nt * LANES), f32),
            pltpu.VMEM((total + 2 * window, 1, nt * LANES), f32),
            pltpu.VMEM((total * rows // LANES, packed, 2 * LANES), bf16),
            pltpu.VMEM((width, per_core * LANES), f32),
            pltpu.VMEM((width, per_core * LANES), f32),
            pltpu.VMEM((nc, 1, width), f32),
            pltpu.VMEM((rows, width), f32),
            pltpu.VMEM((pairs, shard_rows, packed), bf16),
            pltpu.VMEM((nt, nc, nq, wout.shape[0], wout.shape[1]), bf16),
            pltpu.VMEM((total * rows, width), bf16),
            pltpu.VMEM((total * rows, width), bf16),
            pltpu.VMEM((total * rows, packed), f32),
            pltpu.VMEM((total, head_dim, nt * LANES), f32),
            pltpu.VMEM((total + 2 * window, head_dim, nt * LANES), f32),
            pltpu.VMEM((total + 2 * window, head_dim, nt * LANES), f32),
            pltpu.VMEM((pairs, nt, head_dim + tail, LANES), bf16),
            pltpu.VMEM((nt * pairs, head_dim + tail, LANES), bf16),
            pltpu.VMEM((nc, per_core, half, tok_count), f32),
            pltpu.VMEM((per_core, half, tok_count), f32),
            pltpu.VMEM((nc, half, tok_count), f32),
            pltpu.VMEM((half, tok_count), f32),
            dma((2, nq, nt)),
            dma((2, 1)),
            dma((2, 1)),
            dma((2, nq, nc)),
            dma((2, nq)),
            dma((2, nq + 1)),
            dma((2, 2, nq)),
            dma((2, nq)),
            dma((2, 2, nq)),
            dma((2, pairs, nt)),
            dma((2, 1 + nc)),
            dma((4,)),
        ],
        compiler_params=pltpu.CompilerParams(collective_id=0, has_side_effects=True),
    )(
        *staged, *scalars
    )
    return pl.pallas_call(
        hand_on,
        out_shape=(out, out),
        in_specs=[vmem, vmem],
        out_specs=(vmem, vmem),
        scratch_shapes=[],
    )(*results)


def solution(mesh):
    placed = (
        P(("scene", "queue"), None, "tok"),
        P(("scene", "cfg"), "tok"),
        P(("scene", "queue")),
        P(("scene", "queue"), None),
        P(("scene", "cfg"), None),
        P(),
        P(),
        P(("queue", "cfg"), None, "tok"),
        P(),
        P(),
        P("tok", ("queue", "cfg")),
        P(),
        P(),
        P(),
        P(),
    )
    return jax.shard_map(
        on_device,
        mesh=mesh,
        in_specs=placed,
        out_specs=(P(("scene", "queue"), "cfg", "tok"), P(("scene", "queue"), "cfg", "tok")),
        check_vma=False,
    )
```

```python
import functools

import jax
import jax.numpy as jnp
from jax import lax
from jax.experimental import pallas as pl
from jax.experimental.pallas import tpu as pltpu
from jax.sharding import PartitionSpec as P

LANES = 128
HIGH = lax.Precision.HIGHEST

EPS_NORM = 1e-06
TIME_SHIFT = 3.0


def with_halo(cells, sides, width):
    for axis, dim in sides:
        count = lax.axis_size(axis)
        ends = count - 1
        head = lax.slice_in_dim(cells, 0, width, axis=dim)
        tail = lax.slice_in_dim(cells, cells.shape[dim] - width, cells.shape[dim], axis=dim)
        cells = jnp.concatenate(
            [
                lax.ppermute(tail, axis, [(i, (i + 1) % count) for i in range(ends)]),
                cells,
                lax.ppermute(head, axis, [((i + 1) % count, i) for i in range(ends)]),
            ],
            axis=dim,
        )
    return cells


def from_partner(value, axis, bit):
    return lax.ppermute(value, axis, [(i, i ^ 1 << bit) for i in range(lax.axis_size(axis))])


def shifted(value, axis, steps):
    count = lax.axis_size(axis)
    initial, last = (max(0, -steps), min(count, count - steps))
    return lax.ppermute(value, axis, [(source, source + steps) for source in range(initial, last)])


def layer_norm(values):
    center = jnp.mean(values, axis=-1, keepdims=True)
    deviate = values - center
    spread = jnp.mean(deviate * deviate, axis=-1, keepdims=True)
    return deviate * lax.rsqrt(spread + EPS_NORM)


def rms_norm(values, scaling):
    return (
        values * lax.rsqrt(jnp.mean(values * values, axis=-1, keepdims=True) + EPS_NORM) * scaling
    )


def noise_sigma(fraction):
    return TIME_SHIFT * fraction / (1.0 + (TIME_SHIFT - 1.0) * fraction)


def temporal_attention(
    queries, key_rows, value_rows, window_mask, first_frame, total_frames, window
):
    frames = queries.shape[0]
    numerator = jnp.zeros(queries.shape, jnp.float32)
    denominator = jnp.zeros(queries.shape[:-1], jnp.float32)
    for offset in range(2 * window + 1):
        near_keys = key_rows[offset : offset + frames].astype(jnp.float32)
        near_values = value_rows[offset : offset + frames].astype(jnp.float32)
        scores = jnp.sum(queries * near_keys, axis=-1) * queries.shape[-1] ** (-0.5)
        target = first_frame + jnp.arange(frames, dtype=jnp.int32) + (offset - window)
        allowed = (window_mask[:, offset] == 1) & (target >= 0) & (target < total_frames)
        weights = jnp.exp(scores) * allowed.astype(jnp.float32)[:, None, None]
        numerator = numerator + weights[..., None] * near_values
        denominator = denominator + weights
    return numerator / denominator[..., None]


def on_device_plain(
    latents,
    fresh_noise,
    levels,
    window_mask,
    cond_embed,
    level_mod,
    embed_weight,
    qkv_weight,
    query_gain,
    key_gain,
    out_weight,
    final_gain,
    final_weight,
    guide_table,
    guide_index,
):
    frames = latents.shape[0]
    tok_count = latents.shape[2]
    model_width = embed_weight.shape[1]
    head_dim = query_gain.shape[0]
    levels_all = level_mod.shape[0]
    queue_count = lax.axis_size("queue")
    all_tokens = lax.all_gather(latents, "tok", axis=2, tiled=True)
    seq_tokens = all_tokens.shape[2]
    row_count = frames * seq_tokens
    embedded = (
        jnp.einsum(
            "fcs,cd->fsd",
            all_tokens.astype(jnp.bfloat16),
            embed_weight,
            preferred_element_type=jnp.float32,
        )
        + cond_embed[0]
    )
    one_hot = (levels[:, None] == jnp.arange(levels_all, dtype=jnp.int32)[None, :]).astype(
        jnp.float32
    )
    modulate = jnp.dot(
        one_hot, level_mod.reshape(levels_all, 3 * model_width), precision=lax.Precision.HIGHEST
    ).reshape(frames, 3, model_width)
    normed = (layer_norm(embedded) * (1.0 + modulate[:, None, 1]) + modulate[:, None, 0]).astype(
        jnp.bfloat16
    )
    norm_rows = normed.reshape(row_count, model_width)
    local_cols = qkv_weight.shape[2]
    shard_piece = lax.all_gather(qkv_weight, ("queue", "cfg"), axis=0, tiled=True)
    flat_piece = shard_piece.reshape(shard_piece.shape[0], 3 * local_cols)
    projected = jnp.dot(norm_rows, flat_piece, preferred_element_type=jnp.float32)
    projected = projected.reshape(frames, seq_tokens, 3, local_cols // head_dim, head_dim)
    queries = rms_norm(projected[:, :, 0], query_gain)
    keys_values = jnp.stack(
        [
            rms_norm(projected[:, :, 1], key_gain).astype(jnp.bfloat16),
            projected[:, :, 2].astype(jnp.bfloat16),
        ]
    )
    widened = with_halo(keys_values, (("queue", 1),), frames)
    first_frame = lax.axis_index("queue") * frames
    attended = temporal_attention(
        queries, widened[0], widened[1], window_mask, first_frame, frames * queue_count, frames
    )
    attended = attended.astype(jnp.bfloat16).reshape(frames, seq_tokens, local_cols)
    flat_heads = attended.reshape(row_count, local_cols)
    partial_value = jnp.dot(
        flat_heads,
        lax.all_gather(out_weight, ("queue", "cfg"), axis=1, tiled=True),
        preferred_element_type=jnp.float32,
    )
    mixed_out = lax.psum_scatter(
        partial_value.reshape(frames, seq_tokens, model_width).astype(jnp.bfloat16),
        "tok",
        scatter_dimension=1,
        tiled=True,
    ).astype(jnp.float32)
    own_start = lax.axis_index("tok") * tok_count
    own_embed = lax.dynamic_slice_in_dim(embedded, own_start, tok_count, 1)
    summed = own_embed + modulate[:, None, 2] * mixed_out
    final_rows = (layer_norm(summed) * final_gain).astype(jnp.bfloat16)
    velocity = jnp.einsum(
        "ftd,dc->fct", final_rows, final_weight, preferred_element_type=jnp.float32
    )
    half_values = velocity.shape[1] // 2
    branch_index = lax.axis_index("cfg")
    own_first = branch_index * half_values
    other_first = (1 - branch_index) * half_values
    outgoing = lax.dynamic_slice_in_dim(velocity, other_first, half_values, 1)
    partner = from_partner(outgoing, "cfg", 0)
    mine = lax.dynamic_slice_in_dim(velocity, own_first, half_values, 1)
    is_cond = branch_index == 0
    cond_vel = jnp.where(is_cond, mine, partner)
    uncond_vel = jnp.where(is_cond, partner, mine)
    entries = guide_table.shape[0]
    guidance = jnp.sum(
        guide_table * (jnp.arange(entries, dtype=jnp.int32) == guide_index[0]).astype(jnp.float32)
    )
    guided = uncond_vel + guidance * (cond_vel - uncond_vel)
    current = noise_sigma((levels + 1).astype(jnp.float32) / levels_all)
    upcoming = noise_sigma(levels.astype(jnp.float32) / levels_all)
    own_latents = lax.dynamic_slice_in_dim(latents, own_first, half_values, 1)
    updated = own_latents + (upcoming - current)[:, None, None] * guided
    incoming = shifted(updated[:1], "queue", -1)
    is_last = lax.axis_index("queue") == queue_count - 1
    incoming = jnp.where(is_last, fresh_noise[None], incoming)
    new_queue = jnp.concatenate([updated[1:], incoming], axis=0)
    return (guided, new_queue)


def flip(index, mask):
    result, bit = index, 1
    while bit <= mask:
        if mask & bit:
            result = result + bit - 2 * bit * lax.rem(index // bit, 2)
        bit *= 2
    return result


def split2(value):
    high = value.astype(jnp.bfloat16)
    return high, (value - high.astype(jnp.float32)).astype(jnp.bfloat16)


def dot00(left, right, precision=None):
    return lax.dot_general(
        left,
        right,
        (((0,), (0,)), ((), ())),
        precision=precision,
        preferred_element_type=jnp.float32,
    )


def staged_kernel(dims, staged, plain, *refs):
    sources, rest = refs[:staged], refs[staged:]
    others, scratch = rest[: plain + 2], rest[plain + 2 :]
    holders, sems = scratch[:staged], scratch[staged]
    loads = [
        pltpu.make_async_copy(sources[i], holders[i], sems.at[i]) for i in range(staged)
    ]
    for load in loads:
        load.start()
    fused_kernel(dims, loads, *holders, *others, *scratch[staged + 1 :])


def fused_kernel(
    dims,
    loads,
    cond_ref,
    mod_ref,
    embed_ref,
    qkv_ref,
    query_gain_ref,
    key_gain_ref,
    wout_ref,
    final_gain_ref,
    wfinal_ref,
    latents_ref,
    noise_ref,
    table_ref,
    index_ref,
    levels_ref,
    mask_ref,
    guided_ref,
    queue_ref,
    cells_ref,
    wqkv_ref,
    got,
    cells,
    inputs,
    key_scale,
    value_scale,
    proj_t,
    embed_rows,
    gate_rows,
    conds,
    base,
    wq,
    wo,
    scaled_hi,
    scaled_lo,
    proj,
    q_rows,
    k_rows,
    v_rows,
    att_out,
    att_in,
    vel_half,
    vel_got,
    head_half,
    head_got,
    lat_sems,
    cond_sems,
    wq_sems,
    wqz_sems,
    wqy_sems,
    woz_sems,
    woy_sems,
    wox_sems,
    woc_sems,
    att_sems,
    end_sems,
    local_sems,
):
    nq, nt, nc, frames, chans, head_dim, window, tok_count, entries = dims
    span = 2 * window + 1
    total = nq * frames
    per_core = frames // nc
    pairs = nq * nc
    levels_all = mod_ref.shape[1]
    width = embed_ref.shape[1]
    row_level = chans + 4
    rows = cells.shape[2]
    f32, bf16 = jnp.float32, jnp.bfloat16

    s = lax.axis_index("scene")
    q = lax.axis_index("queue")
    t = lax.axis_index("tok")
    c = lax.axis_index("cfg")
    mine = q * nc + c

    barrier = pltpu.get_barrier_semaphore()
    peers = 0
    for dq in range(nq):
        for dt in range(nt):
            for dc in range(nc):
                if dq + dt + dc:
                    peers += 1
                    pl.semaphore_signal(
                        barrier,
                        inc=1,
                        device_id={
                            "queue": lax.rem(q + dq, nq),
                            "tok": lax.rem(t + dt, nt),
                            "cfg": lax.rem(c + dc, nc),
                        },
                        device_id_type=pl.DeviceIdType.MESH,
                    )
    pl.semaphore_signal(
        barrier,
        inc=1,
        device_id={"scene": 1 - s},
        device_id_type=pl.DeviceIdType.MESH,
    )
    for load in loads:
        load.wait()
    gap = LANES - 2 * tok_count
    flag_row = lax.broadcasted_iota(jnp.int32, (chans, gap), 0)
    flag_lane = lax.broadcasted_iota(jnp.int32, (chans, gap), 1)
    for i in range(frames // 2):
        flags = jnp.zeros((chans, gap), f32)
        for h in range(2):
            f = 2 * i + h
            flags = jnp.where(
                (flag_lane == h) & (flag_row == 4), levels_ref[f].astype(f32), flags
            )
            for o in range(span):
                flags = jnp.where(
                    (flag_lane == h) & (flag_row == 5 + o), mask_ref[f, o].astype(f32), flags
                )
        cells_ref[i] = jnp.concatenate(
            [latents_ref[2 * i], latents_ref[2 * i + 1], flags], axis=1
        ).astype(bf16)
    packed = wqkv_ref.shape[2]
    empty = jnp.zeros((qkv_ref.shape[1], packed - 3 * head_dim), f32)
    thirds = [qkv_ref[i].astype(f32) for i in range(3)]
    for j in range(pairs):
        cut = [part[:, j * head_dim : (j + 1) * head_dim] for part in thirds]
        wqkv_ref[j] = jnp.concatenate([*cut, empty], axis=1).astype(bf16)
    inputs[...] = jnp.zeros(inputs.shape, bf16)
    pl.semaphore_wait(barrier, peers + 1)

    def remote(source, target, sems, place, dq, dt, dc, ds=0):
        return pltpu.make_async_remote_copy(
            src_ref=source,
            dst_ref=target,
            send_sem=sems.at[(0, *place)],
            recv_sem=sems.at[(1, *place)],
            device_id={
                "scene": lax.rem(s + ds, 2),
                "queue": lax.rem(q + dq, nq),
                "tok": lax.rem(t + dt, nt),
                "cfg": lax.rem(c + dc, nc),
            },
            device_id_type=pl.DeviceIdType.MESH,
        )

    lat_copies = [
        remote(cells_ref.at[c], got.at[c, t, q], lat_sems, (dq, dt), dq, dt, 0)
        for dq in range(nq)
        for dt in range(nt)
        if dq + dt
    ]
    lat_forward = remote(got.at[c], got.at[c], lat_sems, (0, 0), 0, 0, 1)
    cond_copy = remote(cond_ref, conds.at[c], cond_sems, (0,), 0, 0, 1)
    cond_copy.start()
    for copy in lat_copies:
        copy.start()
    leads = c == s
    near = flip(q, 1)

    def wqz_copy(k, dc):
        peer, core = flip(q, k), lax.rem(c + dc, nc)
        return pltpu.make_async_remote_copy(
            src_ref=wqkv_ref.at[peer * nc + core],
            dst_ref=wq.at[mine],
            send_sem=wqz_sems.at[0, k, dc],
            recv_sem=wqz_sems.at[1, k, c if k == 1 else 0],
            device_id={"queue": peer, "cfg": core},
            device_id_type=pl.DeviceIdType.MESH,
        )

    def near_copy(owner):
        slot = wq.at[near * nc + owner]
        return pltpu.make_async_remote_copy(
            src_ref=slot,
            dst_ref=slot,
            send_sem=wqz_sems.at[0, 0, owner],
            recv_sem=wqz_sems.at[1, 1, owner],
            device_id={"queue": near},
            device_id_type=pl.DeviceIdType.MESH,
        )

    def wqy_copy(k, owner):
        slot = wq.at[flip(q, k) * nc + owner]
        return remote(slot, slot, wqy_sems, (k,), 0, 0, 0, 1)

    places = tuple(flip(q, p) for p in range(nq))
    pieces = len(places)
    shared = (2, 3)

    def piece_of(side, p):
        return wo.at[t if side == 0 else 1 - t, c, places[p]]

    def woz_copy(p):
        return pltpu.make_async_remote_copy(
            src_ref=wout_ref,
            dst_ref=wo.at[t, c, q],
            send_sem=woz_sems.at[0, p],
            recv_sem=woz_sems.at[1, p],
            device_id={"queue": places[p]},
            device_id_type=pl.DeviceIdType.MESH,
        )

    def woy_copy(side, p):
        return remote(piece_of(side, p), piece_of(side, p), woy_sems, (side, p), 0, 0, 0, 1)

    def wox_copy(p):
        return remote(piece_of(0, p) if p else wout_ref, piece_of(0, p), wox_sems, (p,), 0, 1, 0)

    def woc_copy(side, p):
        source = piece_of(side, p) if side or p else wout_ref
        return remote(source, piece_of(side, p), woc_sems, (side, p), 0, 0, 1)

    def arrive(p):
        @pl.when(leads)
        def _():
            woz_copy(p).wait_recv()
            if p in shared:
                wox_copy(p).start()
            woy_copy(0, p).start()

        @pl.when(jnp.logical_not(leads))
        def _():
            woy_copy(0, p).wait_recv()

        if p not in shared:
            wox_copy(p).start()
        woc_copy(0, p).start()

    def arrive_x(p):
        if p in shared:
            @pl.when(leads)
            def _():
                wox_copy(p).wait_recv()
                woy_copy(1, p).start()

            @pl.when(jnp.logical_not(leads))
            def _():
                woy_copy(1, p).wait_recv()
        else:
            wox_copy(p).wait_recv()
        woc_copy(1, p).start()

    @pl.when(leads)
    def _():
        for k in (3, 2):
            for dc in range(nc):
                wqz_copy(k, dc).start()

    @pl.when(leads)
    def _():
        for dc in range(nc):
            wqz_copy(1, dc).start()

    wq_partner = remote(wqkv_ref.at[q * nc + 1 - c], wq.at[mine], wq_sems, (0,), 0, 0, 1)
    wq_partner.start()
    wox_copy(0).start()
    woc_copy(0, 0).start()

    local_copies = [
        pltpu.make_async_copy(cells_ref.at[c], got.at[c, t, q], local_sems.at[0]),
        pltpu.make_async_copy(cond_ref, conds.at[c], local_sems.at[1]),
        pltpu.make_async_copy(wqkv_ref.at[mine], wq.at[mine], local_sems.at[2]),
        pltpu.make_async_copy(wout_ref, wo.at[t, c, q], local_sems.at[3]),
    ]
    for copy in local_copies:
        copy.start()
    blank = jnp.zeros((window, head_dim, nt * LANES), f32)
    k_rows[:window] = blank
    v_rows[:window] = blank
    k_rows[total + window :] = blank
    v_rows[total + window :] = blank
    thin = jnp.zeros((window, 1, nt * LANES), f32)
    for ref in (key_scale, value_scale):
        ref[:window] = thin
        ref[total + window :] = thin
    for copy in local_copies:
        copy.wait()
    cond_copy.wait()
    row_ids = lax.broadcasted_iota(jnp.int32, (rows, 1), 0)
    base[...] = jnp.zeros((rows, width), f32)
    base[:chans] = embed_ref[...].astype(f32)
    base[chans : chans + 1] = conds[0]
    base[chans + 1 : chans + 2] = conds[1]
    plain = base[...]
    centered = plain - jnp.mean(plain, axis=1, keepdims=True)
    gram = lax.dot_general(
        centered,
        centered,
        (((1,), (1,)), ((), ())),
        precision=HIGH,
        preferred_element_type=f32,
    ) * (1.0 / width)

    @pl.when(leads)
    def _():
        pass

    @pl.when(jnp.logical_not(leads))
    def _():
        for dc in range(nc):
            wqz_copy(1, dc).start()

    @pl.when(leads)
    def _():
        woz_copy(1).start()
        for p in range(2, pieces):
            woz_copy(p).start()

    wqz_copy(3, 0).wait_recv()
    wqy_copy(3, s).start()
    for copy in lat_copies:
        copy.wait()
    lat_forward.start()
    lat_forward.wait()

    extra = lax.broadcasted_iota(jnp.int32, (chans, LANES), 0)
    lane = lax.broadcasted_iota(jnp.int32, (chans, LANES), 1)
    first = (extra == 0) & (lane < tok_count)
    second = (extra == 1) & (lane >= tok_count) & (lane < 2 * tok_count)
    marks = jnp.where(first | second, 1.0, 0.0)

    def unpack(i, carry):
        for side in range(nt):
            block = got[lax.rem(i, nc), side, i // nc].astype(f32)
            for h in range(2):
                tokens = block[:, h * tok_count : (h + 1) * tok_count]
                spread = jnp.concatenate([tokens, tokens, jnp.zeros((chans, gap), f32)], axis=1)
                flag = block[:, 2 * tok_count + h : 2 * tok_count + h + 1]
                cells[side, 2 * i + h, :chans] = spread.astype(bf16)
                cells[side, 2 * i + h, chans:] = (marks + flag).astype(bf16)
        return carry

    lax.fori_loop(0, total // 2, unpack, 0)

    level_column = cells[0, :, row_level, :].astype(f32)
    level_ids = lax.broadcasted_iota(jnp.int32, (total, LANES), 1).astype(f32)
    one_hot = (level_column == level_ids).astype(f32)[:, :levels_all]
    shift = jnp.dot(one_hot, mod_ref[0], precision=HIGH, preferred_element_type=f32)
    scale = jnp.dot(one_hot, mod_ref[1], precision=HIGH, preferred_element_type=f32) + 1.0
    is_shift = (row_ids == chans + 2) | (row_ids == chans + 3)
    for f in range(total):
        block = jnp.where(is_shift, shift[f : f + 1], centered * scale[f : f + 1])
        high, low = split2(block)
        scaled_hi[f * rows : (f + 1) * rows] = high
        scaled_lo[f * rows : (f + 1) * rows] = low

    group = LANES // rows

    def frame_cells(f):
        return jnp.concatenate([cells[i, f].astype(f32) for i in range(nt)], axis=1)

    def prepare(f, carry):
        cell = jnp.where(row_ids < chans + 2, frame_cells(f), 0.0)
        spread = jnp.sum(
            cell * jnp.dot(gram, cell, precision=HIGH, preferred_element_type=f32),
            axis=0,
            keepdims=True,
        )
        spread = jnp.maximum(spread, 0.0) + EPS_NORM
        inverse = lax.rsqrt(spread)
        sigma = spread * inverse
        sigma_hi = sigma.astype(bf16).astype(f32)
        cell = jnp.where(row_ids == chans + 2, sigma_hi, cell)
        cell = jnp.where(row_ids == chans + 3, sigma - sigma_hi, cell)
        low_row = pl.multiple_of(lax.rem(f, group) * rows, rows)
        inputs[f, pl.ds(low_row, rows)] = cell.astype(bf16)
        inputs[f, pl.ds(low_row + LANES, rows)] = cell.astype(bf16)
        value_scale[f + window] = inverse
        return carry

    lax.fori_loop(0, total // 2, prepare, 0, unroll=4)
    lax.fori_loop(total // 2, total, prepare, 0, unroll=4)
    arrive_x(0)
    wqz_copy(2, 0).wait_recv()
    wqy_copy(2, s).start()


    arrive(1)
    own_lanes = 2 * tok_count
    rest_lanes = 2 * own_lanes - LANES
    tail = att_out.shape[2] - head_dim
    lane_ids = lax.broadcasted_iota(jnp.int32, (1, LANES), 1)
    own_lane = lane_ids < own_lanes
    rest_lane = lane_ids < rest_lanes

    def join(low, high):
        rest = pltpu.roll(high, own_lanes, 1)
        return jnp.concatenate([jnp.where(own_lane, low, rest), rest], axis=1)

    own = join(*[cells[t, mine * per_core + i].astype(f32) for i in range(per_core)])
    embed_rows[...] = dot00(plain, jnp.where(row_ids < chans + 2, own, 0.0), HIGH)
    own_level = own[row_level : row_level + 1]
    own_hot = (
        own_level == lax.broadcasted_iota(jnp.int32, (levels_all, 1), 0).astype(f32)
    ).astype(f32)
    gate_rows[...] = dot00(mod_ref[2], own_hot, HIGH)

    wq_partner.wait()
    for k in (3, 2):
        wqy_copy(k, 1 - s).wait_recv()
    near_copy(0).wait_recv()
    near_copy(1).wait_recv()
    weights = wq[...].reshape(width, wq.shape[2])
    proj[...] = jnp.dot(scaled_hi[...], weights, preferred_element_type=f32) + jnp.dot(
        scaled_lo[...], weights, preferred_element_type=f32
    )

    diagonal = lax.broadcasted_iota(jnp.int32, (head_dim, head_dim), 0) == (
        lax.broadcasted_iota(jnp.int32, (head_dim, head_dim), 1)
    )

    def column(gain_ref):
        return jnp.sum(jnp.where(diagonal, gain_ref[...], 0.0), axis=1, keepdims=True)

    gain = column(query_gain_ref) * column(key_gain_ref) * head_dim**-0.5
    for g in range(total // group):
        block = proj[g * LANES : (g + 1) * LANES].T
        high, low = split2(block)
        proj_t[g] = jnp.concatenate([high, low], axis=1)

    def project(f, carry):
        whole = jnp.dot(proj_t[f // group], inputs[f], preferred_element_type=f32)
        inverse = value_scale[f + window]
        query = whole[:head_dim]
        key = whole[head_dim : 2 * head_dim]

        def rms(part):
            spread = jnp.mean(part * part, axis=0, keepdims=True)
            return inverse * lax.rsqrt(spread * inverse * inverse + EPS_NORM)

        q_rows[f] = query * gain * rms(query)
        k_rows[f + window] = key
        key_scale[f + window] = rms(key)
        v_rows[f + window] = whole[2 * head_dim : 3 * head_dim]
        return carry

    lax.fori_loop(0, total // 2, project, 0, unroll=4)
    arrive(2)
    lax.fori_loop(total // 2, total, project, 0, unroll=4)
    arrive_x(1)
    arrive(3)
    def attend(pair):
        done = []
        for inner in range(per_core):
            f = pair * per_core + inner
            cell = frame_cells(f)
            query = q_rows[f]
            numerator = jnp.zeros((head_dim, nt * LANES), f32)
            denominator = jnp.zeros((1, nt * LANES), f32)
            for o in range(span):
                score = jnp.sum(query * k_rows[f + o], axis=0, keepdims=True)
                row = row_level + 1 + o
                weight = jnp.exp(score * key_scale[f + o]) * cell[row : row + 1]
                numerator = numerator + (weight * value_scale[f + o]) * v_rows[f + o]
                denominator = denominator + weight
            done.append(numerator / denominator)
        for i in range(nt):
            low, high = (d[:, i * LANES : (i + 1) * LANES] for d in done)
            rest = pltpu.roll(high, own_lanes, 1)
            joined = jnp.where(own_lane, low, rest)
            upper = pltpu.roll(rest[head_dim - tail :], rest_lanes, 1)
            folded = jnp.where(rest_lane, rest[:tail], upper)
            att_out[pair, i] = jnp.concatenate([joined, folded], axis=0).astype(bf16)

    head = t * pairs + mine

    def att_copy(step, dt):
        pair = lax.rem(mine + step, pairs)
        other = lax.rem(t + dt, nt)
        return pltpu.make_async_remote_copy(
            src_ref=att_out.at[pair, other],
            dst_ref=att_in.at[head],
            send_sem=att_sems.at[0, step, dt],
            recv_sem=att_sems.at[1, step, dt],
            device_id={"queue": pair // nc, "tok": other, "cfg": lax.rem(pair, nc)},
            device_id_type=pl.DeviceIdType.MESH,
        )

    def attend_step(step, carry):
        attend(lax.rem(mine + step, pairs))
        for dt in range(nt):
            att_copy(step, dt).start()
        return carry

    lax.fori_loop(1, pairs, attend_step, 0)
    attend(mine)
    for dt in range(1, nt):
        att_copy(0, dt).start()
    att_in[head] = att_out[mine, t]

    arrive_x(2)
    arrive_x(3)

    def att_wait(step, carry):
        for dt in range(nt):
            att_copy(step, dt).wait()
        return carry

    lax.fori_loop(1, pairs, att_wait, 0)
    for dt in range(1, nt):
        att_copy(0, dt).wait()
    for p in range(pieces):
        woc_copy(0, p).wait()
        woc_copy(1, p).wait()
    for p in range(pieces):
        if p not in shared:
            wox_copy(p).wait_send()

    group = pairs * head_dim
    arrived = att_in[...].astype(f32)
    folded = arrived[:, head_dim:]
    upper = pltpu.roll(folded[:, 2 * tail - head_dim :], LANES - rest_lanes, 2)
    attended = jnp.concatenate(
        [arrived[:, :head_dim], jnp.concatenate([folded, upper], axis=1)], axis=2
    )
    attended = attended.reshape(nt * group, 2 * LANES).astype(bf16)
    slices = []
    for i in range(nt):
        by_core = [
            jnp.dot(
                wo[i, k].reshape(nq * wo.shape[3], group),
                attended[i * group : (i + 1) * group],
                preferred_element_type=f32,
            )
            for k in range(nc)
        ]
        slices.append(by_core)
    piece = wo.shape[3]
    mixed = jnp.concatenate(
        [
            sum(slices[i][k][j * piece : (j + 1) * piece] for i in range(nt))
            for j in range(nq)
            for k in range(nc)
        ],
        axis=0,
    )
    summed = embed_rows[...] + gate_rows[...] * mixed
    deviate = summed - jnp.mean(summed, axis=0, keepdims=True)
    inverse = lax.rsqrt(jnp.mean(deviate * deviate, axis=0, keepdims=True) + EPS_NORM)
    rounded = deviate.astype(bf16)
    final_hi, final_lo = split2(
        wfinal_ref[...].astype(f32)
        * jnp.concatenate([final_gain_ref[i : i + 1] for i in range(width // LANES)], axis=1)
    )
    velocity = (
        jnp.dot(final_hi, rounded, preferred_element_type=f32)
        + jnp.dot(final_lo, rounded, preferred_element_type=f32)
    ) * inverse

    guidance = jnp.float32(0.0)
    for i in range(entries):
        guidance = guidance + jnp.where(index_ref[0] == i, table_ref[i], 0.0)

    def step_of(level):
        upcoming = noise_sigma(level / levels_all)
        current = noise_sigma((level + 1.0) / levels_all)
        return upcoming - current

    half = chans // nc
    for i in range(per_core):
        begin = i * own_lanes
        cond_vel = velocity[:, begin : begin + tok_count]
        uncond_vel = velocity[:, begin + tok_count : begin + 2 * tok_count]
        guided = uncond_vel + guidance * (cond_vel - uncond_vel)
        for k in range(nc):
            vel_half[k, i] = guided[k * half : (k + 1) * half]
        if i == 0:
            change = step_of(own_level[:, :tok_count])
            updated = latents_ref[0] + change * guided
            for k in range(nc):
                head_half[k] = updated[k * half : (k + 1) * half]

    own_slot = pl.ds(c * per_core, per_core)
    vel_copy = remote(vel_half.at[1 - c], vel_got, end_sems, (0,), 0, 0, 1)
    vel_copy.start()

    def head_copy(k):
        return pltpu.make_async_remote_copy(
            src_ref=head_half.at[k],
            dst_ref=head_got,
            send_sem=end_sems.at[0, 1 + k],
            recv_sem=end_sems.at[1, 1],
            device_id={"queue": lax.rem(q + nq - 1, nq), "cfg": k},
            device_id_type=pl.DeviceIdType.MESH,
        )

    @pl.when((c == 0) & (q > 0))
    def _():
        for k in range(nc):
            head_copy(k).start()

    guided_ref[own_slot] = vel_half[c]
    vel_copy.wait()
    guided_ref[pl.ds((1 - c) * per_core, per_core)] = vel_got[...]
    own_half = pl.ds(pl.multiple_of(c * half, half), half)
    for f in range(1, frames):
        level = cells[t, q * frames + f].astype(f32)[row_level : row_level + 1, :tok_count]
        queue_ref[f - 1] = latents_ref[f, own_half] + step_of(level) * guided_ref[f]

    @pl.when(q == nq - 1)
    def _():
        queue_ref[frames - 1] = noise_ref[...]

    @pl.when(q < nq - 1)
    def _():
        head_copy(0).wait_recv()
        queue_ref[frames - 1] = head_got[...]

    @pl.when((c == 0) & (q > 0))
    def _():
        for k in range(nc):
            head_copy(k).wait_send()

    for k in (3, 2):
        wqy_copy(k, s).wait_send()

    @pl.when(jnp.logical_not(leads))
    def _():
        for dc in range(nc):
            wqz_copy(1, dc).wait_send()

    @pl.when(leads)
    def _():
        for k in range(1, nq):
            for dc in range(nc):
                wqz_copy(k, dc).wait_send()
        for p in range(1, pieces):
            woz_copy(p).wait_send()
            woy_copy(0, p).wait_send()
            if p in shared:
                wox_copy(p).wait_send()
                woy_copy(1, p).wait_send()


def hand_on(guided_ref, queue_ref, guided_out, queue_out):
    guided_out[...] = guided_ref[...]
    queue_out[...] = queue_ref[...]


def on_device(
    latents,
    fresh_noise,
    levels,
    window_mask,
    cond_embed,
    level_mod,
    embed_weight,
    qkv_weight,
    query_gain,
    key_gain,
    out_weight,
    final_gain,
    final_weight,
    guide_table,
    guide_index,
):
    frames, chans, tok_count = latents.shape
    width = embed_weight.shape[1]
    head_dim = query_gain.shape[0]
    levels_all = level_mod.shape[0]
    nq, nt, nc = (lax.axis_size(a) for a in ("queue", "tok", "cfg"))
    shard_rows, _, local_cols = qkv_weight.shape
    pairs = nq * nc
    span = window_mask.shape[1]
    window = span // 2
    rows = 2 * chans
    fits = (
        local_cols == pairs * head_dim
        and frames % nc == 0
        and frames % 2 == 0
        and chans >= 5 + span
        and 2 * tok_count + 2 <= LANES
        and nc == 2
        and nt == 2
        and lax.axis_size("scene") == 2
        and chans % (8 * nc) == 0
        and 2 * tok_count <= LANES
        and levels_all <= LANES
        and nq == 4
        and width % LANES == 0
        and frames == 2 * nc
        and 4 * tok_count == LANES + LANES // 2
        and frames == LANES // rows
    )
    if not fits:
        return on_device_plain(
            latents, fresh_noise, levels, window_mask, cond_embed, level_mod, embed_weight,
            qkv_weight, query_gain, key_gain, out_weight, final_gain, final_weight,
            guide_table, guide_index,
        )
    f32, bf16 = jnp.float32, jnp.bfloat16
    packed = -(-3 * head_dim // LANES) * LANES
    wqkv = qkv_weight.transpose(1, 0, 2)
    wout = out_weight.T
    wfinal = final_weight.T
    mods = level_mod.transpose(1, 0, 2)
    total = nq * frames
    per_core = frames // nc
    half = chans // nc
    tail = -(-head_dim // 16) * 8
    dims = (nq, nt, nc, frames, chans, head_dim, window, tok_count, guide_table.shape[0])
    vmem = pl.BlockSpec(memory_space=pltpu.VMEM)
    smem = pl.BlockSpec(memory_space=pltpu.SMEM)
    dma = pltpu.SemaphoreType.DMA
    out = jax.ShapeDtypeStruct((frames, half, tok_count), f32)
    staged = [
        cond_embed, mods, embed_weight, wqkv, query_gain[None], key_gain[None], wout,
        final_gain.reshape(width // LANES, LANES), wfinal, latents, fresh_noise,
    ]
    scalars = [guide_table, guide_index, levels, window_mask]
    anywhere = pl.BlockSpec(memory_space=pl.ANY)
    results = pl.pallas_call(
        functools.partial(staged_kernel, dims, len(staged), len(scalars)),
        out_shape=(out, out),
        in_specs=[anywhere] * len(staged) + [smem] * len(scalars),
        out_specs=(vmem, vmem),
        scratch_shapes=[
            *[pltpu.VMEM(array.shape, array.dtype) for array in staged],
            dma((len(staged),)),
            pltpu.VMEM((frames // 2, chans, LANES), bf16),
            pltpu.VMEM((pairs, shard_rows, packed), bf16),
            pltpu.VMEM((nc, nt, nq, chans, LANES), bf16),
            pltpu.VMEM((nt, total, rows, LANES), bf16),
            pltpu.VMEM((total, 2 * LANES, nt * LANES), bf16),
            pltpu.VMEM((total + 2 * window, 1, nt * LANES), f32),
            pltpu.VMEM((total + 2 * window, 1, nt * LANES), f32),
            pltpu.VMEM((total * rows // LANES, packed, 2 * LANES), bf16),
            pltpu.VMEM((width, per_core * LANES), f32),
            pltpu.VMEM((width, per_core * LANES), f32),
            pltpu.VMEM((nc, 1, width), f32),
            pltpu.VMEM((rows, width), f32),
            pltpu.VMEM((pairs, shard_rows, packed), bf16),
            pltpu.VMEM((nt, nc, nq, wout.shape[0], wout.shape[1]), bf16),
            pltpu.VMEM((total * rows, width), bf16),
            pltpu.VMEM((total * rows, width), bf16),
            pltpu.VMEM((total * rows, packed), f32),
            pltpu.VMEM((total, head_dim, nt * LANES), f32),
            pltpu.VMEM((total + 2 * window, head_dim, nt * LANES), f32),
            pltpu.VMEM((total + 2 * window, head_dim, nt * LANES), f32),
            pltpu.VMEM((pairs, nt, head_dim + tail, LANES), bf16),
            pltpu.VMEM((nt * pairs, head_dim + tail, LANES), bf16),
            pltpu.VMEM((nc, per_core, half, tok_count), f32),
            pltpu.VMEM((per_core, half, tok_count), f32),
            pltpu.VMEM((nc, half, tok_count), f32),
            pltpu.VMEM((half, tok_count), f32),
            dma((2, nq, nt)),
            dma((2, 1)),
            dma((2, 1)),
            dma((2, nq, nc)),
            dma((2, nq)),
            dma((2, nq + 1)),
            dma((2, 2, nq)),
            dma((2, nq)),
            dma((2, 2, nq)),
            dma((2, pairs, nt)),
            dma((2, 1 + nc)),
            dma((4,)),
        ],
        compiler_params=pltpu.CompilerParams(collective_id=0, has_side_effects=True),
    )(
        *staged, *scalars
    )
    return pl.pallas_call(
        hand_on,
        out_shape=(out, out),
        in_specs=[vmem, vmem],
        out_specs=(vmem, vmem),
        scratch_shapes=[],
    )(*results)


def solution(mesh):
    placed = (
        P(("scene", "queue"), None, "tok"),
        P(("scene", "cfg"), "tok"),
        P(("scene", "queue")),
        P(("scene", "queue"), None),
        P(("scene", "cfg"), None),
        P(),
        P(),
        P(("queue", "cfg"), None, "tok"),
        P(),
        P(),
        P("tok", ("queue", "cfg")),
        P(),
        P(),
        P(),
        P(),
    )
    return jax.shard_map(
        on_device,
        mesh=mesh,
        in_specs=placed,
        out_specs=(P(("scene", "queue"), "cfg", "tok"), P(("scene", "queue"), "cfg", "tok")),
        check_vma=False,
    )
```

```python
import functools

import jax
import jax.numpy as jnp
from jax import lax
from jax.experimental import pallas as pl
from jax.experimental.pallas import tpu as pltpu
from jax.sharding import PartitionSpec as P

LANES = 128
HIGH = lax.Precision.HIGHEST

EPS_NORM = 1e-06
TIME_SHIFT = 3.0


def with_halo(cells, sides, width):
    for axis, dim in sides:
        count = lax.axis_size(axis)
        ends = count - 1
        head = lax.slice_in_dim(cells, 0, width, axis=dim)
        tail = lax.slice_in_dim(cells, cells.shape[dim] - width, cells.shape[dim], axis=dim)
        cells = jnp.concatenate(
            [
                lax.ppermute(tail, axis, [(i, (i + 1) % count) for i in range(ends)]),
                cells,
                lax.ppermute(head, axis, [((i + 1) % count, i) for i in range(ends)]),
            ],
            axis=dim,
        )
    return cells


def from_partner(value, axis, bit):
    return lax.ppermute(value, axis, [(i, i ^ 1 << bit) for i in range(lax.axis_size(axis))])


def shifted(value, axis, steps):
    count = lax.axis_size(axis)
    initial, last = (max(0, -steps), min(count, count - steps))
    return lax.ppermute(value, axis, [(source, source + steps) for source in range(initial, last)])


def layer_norm(values):
    center = jnp.mean(values, axis=-1, keepdims=True)
    deviate = values - center
    spread = jnp.mean(deviate * deviate, axis=-1, keepdims=True)
    return deviate * lax.rsqrt(spread + EPS_NORM)


def rms_norm(values, scaling):
    return (
        values * lax.rsqrt(jnp.mean(values * values, axis=-1, keepdims=True) + EPS_NORM) * scaling
    )


def noise_sigma(fraction):
    return TIME_SHIFT * fraction / (1.0 + (TIME_SHIFT - 1.0) * fraction)


def temporal_attention(
    queries, key_rows, value_rows, window_mask, first_frame, total_frames, window
):
    frames = queries.shape[0]
    numerator = jnp.zeros(queries.shape, jnp.float32)
    denominator = jnp.zeros(queries.shape[:-1], jnp.float32)
    for offset in range(2 * window + 1):
        near_keys = key_rows[offset : offset + frames].astype(jnp.float32)
        near_values = value_rows[offset : offset + frames].astype(jnp.float32)
        scores = jnp.sum(queries * near_keys, axis=-1) * queries.shape[-1] ** (-0.5)
        target = first_frame + jnp.arange(frames, dtype=jnp.int32) + (offset - window)
        allowed = (window_mask[:, offset] == 1) & (target >= 0) & (target < total_frames)
        weights = jnp.exp(scores) * allowed.astype(jnp.float32)[:, None, None]
        numerator = numerator + weights[..., None] * near_values
        denominator = denominator + weights
    return numerator / denominator[..., None]


def on_device_plain(
    latents,
    fresh_noise,
    levels,
    window_mask,
    cond_embed,
    level_mod,
    embed_weight,
    qkv_weight,
    query_gain,
    key_gain,
    out_weight,
    final_gain,
    final_weight,
    guide_table,
    guide_index,
):
    frames = latents.shape[0]
    tok_count = latents.shape[2]
    model_width = embed_weight.shape[1]
    head_dim = query_gain.shape[0]
    levels_all = level_mod.shape[0]
    queue_count = lax.axis_size("queue")
    all_tokens = lax.all_gather(latents, "tok", axis=2, tiled=True)
    seq_tokens = all_tokens.shape[2]
    row_count = frames * seq_tokens
    embedded = (
        jnp.einsum(
            "fcs,cd->fsd",
            all_tokens.astype(jnp.bfloat16),
            embed_weight,
            preferred_element_type=jnp.float32,
        )
        + cond_embed[0]
    )
    one_hot = (levels[:, None] == jnp.arange(levels_all, dtype=jnp.int32)[None, :]).astype(
        jnp.float32
    )
    modulate = jnp.dot(
        one_hot, level_mod.reshape(levels_all, 3 * model_width), precision=lax.Precision.HIGHEST
    ).reshape(frames, 3, model_width)
    normed = (layer_norm(embedded) * (1.0 + modulate[:, None, 1]) + modulate[:, None, 0]).astype(
        jnp.bfloat16
    )
    norm_rows = normed.reshape(row_count, model_width)
    local_cols = qkv_weight.shape[2]
    shard_piece = lax.all_gather(qkv_weight, ("queue", "cfg"), axis=0, tiled=True)
    flat_piece = shard_piece.reshape(shard_piece.shape[0], 3 * local_cols)
    projected = jnp.dot(norm_rows, flat_piece, preferred_element_type=jnp.float32)
    projected = projected.reshape(frames, seq_tokens, 3, local_cols // head_dim, head_dim)
    queries = rms_norm(projected[:, :, 0], query_gain)
    keys_values = jnp.stack(
        [
            rms_norm(projected[:, :, 1], key_gain).astype(jnp.bfloat16),
            projected[:, :, 2].astype(jnp.bfloat16),
        ]
    )
    widened = with_halo(keys_values, (("queue", 1),), frames)
    first_frame = lax.axis_index("queue") * frames
    attended = temporal_attention(
        queries, widened[0], widened[1], window_mask, first_frame, frames * queue_count, frames
    )
    attended = attended.astype(jnp.bfloat16).reshape(frames, seq_tokens, local_cols)
    flat_heads = attended.reshape(row_count, local_cols)
    partial_value = jnp.dot(
        flat_heads,
        lax.all_gather(out_weight, ("queue", "cfg"), axis=1, tiled=True),
        preferred_element_type=jnp.float32,
    )
    mixed_out = lax.psum_scatter(
        partial_value.reshape(frames, seq_tokens, model_width).astype(jnp.bfloat16),
        "tok",
        scatter_dimension=1,
        tiled=True,
    ).astype(jnp.float32)
    own_start = lax.axis_index("tok") * tok_count
    own_embed = lax.dynamic_slice_in_dim(embedded, own_start, tok_count, 1)
    summed = own_embed + modulate[:, None, 2] * mixed_out
    final_rows = (layer_norm(summed) * final_gain).astype(jnp.bfloat16)
    velocity = jnp.einsum(
        "ftd,dc->fct", final_rows, final_weight, preferred_element_type=jnp.float32
    )
    half_values = velocity.shape[1] // 2
    branch_index = lax.axis_index("cfg")
    own_first = branch_index * half_values
    other_first = (1 - branch_index) * half_values
    outgoing = lax.dynamic_slice_in_dim(velocity, other_first, half_values, 1)
    partner = from_partner(outgoing, "cfg", 0)
    mine = lax.dynamic_slice_in_dim(velocity, own_first, half_values, 1)
    is_cond = branch_index == 0
    cond_vel = jnp.where(is_cond, mine, partner)
    uncond_vel = jnp.where(is_cond, partner, mine)
    entries = guide_table.shape[0]
    guidance = jnp.sum(
        guide_table * (jnp.arange(entries, dtype=jnp.int32) == guide_index[0]).astype(jnp.float32)
    )
    guided = uncond_vel + guidance * (cond_vel - uncond_vel)
    current = noise_sigma((levels + 1).astype(jnp.float32) / levels_all)
    upcoming = noise_sigma(levels.astype(jnp.float32) / levels_all)
    own_latents = lax.dynamic_slice_in_dim(latents, own_first, half_values, 1)
    updated = own_latents + (upcoming - current)[:, None, None] * guided
    incoming = shifted(updated[:1], "queue", -1)
    is_last = lax.axis_index("queue") == queue_count - 1
    incoming = jnp.where(is_last, fresh_noise[None], incoming)
    new_queue = jnp.concatenate([updated[1:], incoming], axis=0)
    return (guided, new_queue)


def flip(index, mask):
    result, bit = index, 1
    while bit <= mask:
        if mask & bit:
            result = result + bit - 2 * bit * lax.rem(index // bit, 2)
        bit *= 2
    return result


def split2(value):
    high = value.astype(jnp.bfloat16)
    return high, (value - high.astype(jnp.float32)).astype(jnp.bfloat16)


def dot00(left, right, precision=None):
    return lax.dot_general(
        left,
        right,
        (((0,), (0,)), ((), ())),
        precision=precision,
        preferred_element_type=jnp.float32,
    )


def staged_kernel(dims, staged, plain, *refs):
    sources, rest = refs[:staged], refs[staged:]
    others, scratch = rest[: plain + 2], rest[plain + 2 :]
    holders, sems = scratch[:staged], scratch[staged]
    loads = [
        pltpu.make_async_copy(sources[i], holders[i], sems.at[i]) for i in range(staged)
    ]
    for load in loads:
        load.start()
    fused_kernel(dims, loads, *holders, *others, *scratch[staged + 1 :])


def fused_kernel(
    dims,
    loads,
    cond_ref,
    mod_ref,
    embed_ref,
    qkv_ref,
    query_gain_ref,
    key_gain_ref,
    wout_ref,
    final_gain_ref,
    wfinal_ref,
    latents_ref,
    noise_ref,
    table_ref,
    index_ref,
    levels_ref,
    mask_ref,
    guided_ref,
    queue_ref,
    cells_ref,
    wqkv_ref,
    got,
    cells,
    inputs,
    key_scale,
    value_scale,
    proj_t,
    embed_rows,
    gate_rows,
    conds,
    base,
    wq,
    wo,
    scaled_hi,
    scaled_lo,
    proj,
    q_rows,
    k_rows,
    v_rows,
    att_out,
    att_in,
    vel_half,
    vel_got,
    head_half,
    head_got,
    lat_sems,
    cond_sems,
    wq_sems,
    wqz_sems,
    wqy_sems,
    woz_sems,
    woy_sems,
    wox_sems,
    woc_sems,
    att_sems,
    end_sems,
    local_sems,
):
    nq, nt, nc, frames, chans, head_dim, window, tok_count, entries = dims
    span = 2 * window + 1
    total = nq * frames
    per_core = frames // nc
    pairs = nq * nc
    levels_all = mod_ref.shape[1]
    width = embed_ref.shape[1]
    row_level = chans + 4
    rows = cells.shape[2]
    f32, bf16 = jnp.float32, jnp.bfloat16

    s = lax.axis_index("scene")
    q = lax.axis_index("queue")
    t = lax.axis_index("tok")
    c = lax.axis_index("cfg")
    mine = q * nc + c

    barrier = pltpu.get_barrier_semaphore()
    peers = 0
    for dq in range(nq):
        for dt in range(nt):
            for dc in range(nc):
                if dq + dt + dc:
                    peers += 1
                    pl.semaphore_signal(
                        barrier,
                        inc=1,
                        device_id={
                            "queue": lax.rem(q + dq, nq),
                            "tok": lax.rem(t + dt, nt),
                            "cfg": lax.rem(c + dc, nc),
                        },
                        device_id_type=pl.DeviceIdType.MESH,
                    )
    pl.semaphore_signal(
        barrier,
        inc=1,
        device_id={"scene": 1 - s},
        device_id_type=pl.DeviceIdType.MESH,
    )
    for load in loads:
        load.wait()
    gap = LANES - 2 * tok_count
    flag_row = lax.broadcasted_iota(jnp.int32, (chans, gap), 0)
    flag_lane = lax.broadcasted_iota(jnp.int32, (chans, gap), 1)
    for i in range(frames // 2):
        flags = jnp.zeros((chans, gap), f32)
        for h in range(2):
            f = 2 * i + h
            flags = jnp.where(
                (flag_lane == h) & (flag_row == 4), levels_ref[f].astype(f32), flags
            )
            for o in range(span):
                flags = jnp.where(
                    (flag_lane == h) & (flag_row == 5 + o), mask_ref[f, o].astype(f32), flags
                )
        cells_ref[i] = jnp.concatenate(
            [latents_ref[2 * i], latents_ref[2 * i + 1], flags], axis=1
        ).astype(bf16)
    packed = wqkv_ref.shape[2]
    empty = jnp.zeros((qkv_ref.shape[1], packed - 3 * head_dim), f32)
    thirds = [qkv_ref[i].astype(f32) for i in range(3)]
    for j in range(pairs):
        cut = [part[:, j * head_dim : (j + 1) * head_dim] for part in thirds]
        wqkv_ref[j] = jnp.concatenate([*cut, empty], axis=1).astype(bf16)
    inputs[...] = jnp.zeros(inputs.shape, bf16)
    pl.semaphore_wait(barrier, peers + 1)

    def remote(source, target, sems, place, dq, dt, dc, ds=0):
        return pltpu.make_async_remote_copy(
            src_ref=source,
            dst_ref=target,
            send_sem=sems.at[(0, *place)],
            recv_sem=sems.at[(1, *place)],
            device_id={
                "scene": lax.rem(s + ds, 2),
                "queue": lax.rem(q + dq, nq),
                "tok": lax.rem(t + dt, nt),
                "cfg": lax.rem(c + dc, nc),
            },
            device_id_type=pl.DeviceIdType.MESH,
        )

    lat_copies = [
        remote(cells_ref.at[c], got.at[c, t, q], lat_sems, (dq, dt), dq, dt, 0)
        for dq in range(nq)
        for dt in range(nt)
        if dq + dt
    ]
    lat_forward = remote(got.at[c], got.at[c], lat_sems, (0, 0), 0, 0, 1)
    cond_copy = remote(cond_ref, conds.at[c], cond_sems, (0,), 0, 0, 1)
    cond_copy.start()
    for copy in lat_copies:
        copy.start()
    leads = c == s
    near = flip(q, 1)

    def wqz_copy(k, dc):
        peer, core = flip(q, k), lax.rem(c + dc, nc)
        return pltpu.make_async_remote_copy(
            src_ref=wqkv_ref.at[peer * nc + core],
            dst_ref=wq.at[mine],
            send_sem=wqz_sems.at[0, k, dc],
            recv_sem=wqz_sems.at[1, k, c if k == 1 else 0],
            device_id={"queue": peer, "cfg": core},
            device_id_type=pl.DeviceIdType.MESH,
        )

    def near_copy(owner):
        slot = wq.at[near * nc + owner]
        return pltpu.make_async_remote_copy(
            src_ref=slot,
            dst_ref=slot,
            send_sem=wqz_sems.at[0, 0, owner],
            recv_sem=wqz_sems.at[1, 1, owner],
            device_id={"queue": near},
            device_id_type=pl.DeviceIdType.MESH,
        )

    def wqy_copy(k, owner):
        slot = wq.at[flip(q, k) * nc + owner]
        return remote(slot, slot, wqy_sems, (k,), 0, 0, 0, 1)

    places = tuple(flip(q, p) for p in range(nq))
    pieces = len(places)
    shared = (2, 3)

    def piece_of(side, p):
        return wo.at[t if side == 0 else 1 - t, c, places[p]]

    def woz_copy(p):
        return pltpu.make_async_remote_copy(
            src_ref=wout_ref,
            dst_ref=wo.at[t, c, q],
            send_sem=woz_sems.at[0, p],
            recv_sem=woz_sems.at[1, p],
            device_id={"queue": places[p]},
            device_id_type=pl.DeviceIdType.MESH,
        )

    def woy_copy(side, p):
        return remote(piece_of(side, p), piece_of(side, p), woy_sems, (side, p), 0, 0, 0, 1)

    def wox_copy(p):
        return remote(piece_of(0, p) if p else wout_ref, piece_of(0, p), wox_sems, (p,), 0, 1, 0)

    def woc_copy(side, p):
        source = piece_of(side, p) if side or p else wout_ref
        return remote(source, piece_of(side, p), woc_sems, (side, p), 0, 0, 1)

    def arrive(p):
        @pl.when(leads)
        def _():
            woz_copy(p).wait_recv()
            if p in shared:
                wox_copy(p).start()
            woy_copy(0, p).start()

        @pl.when(jnp.logical_not(leads))
        def _():
            woy_copy(0, p).wait_recv()

        if p not in shared:
            wox_copy(p).start()
        woc_copy(0, p).start()

    def arrive_x(p):
        if p in shared:
            @pl.when(leads)
            def _():
                wox_copy(p).wait_recv()
                woy_copy(1, p).start()

            @pl.when(jnp.logical_not(leads))
            def _():
                woy_copy(1, p).wait_recv()
        else:
            wox_copy(p).wait_recv()
        woc_copy(1, p).start()

    @pl.when(leads)
    def _():
        for k in (3, 2):
            for dc in range(nc):
                wqz_copy(k, dc).start()

    @pl.when(leads)
    def _():
        for dc in range(nc):
            wqz_copy(1, dc).start()

    wq_partner = remote(wqkv_ref.at[q * nc + 1 - c], wq.at[mine], wq_sems, (0,), 0, 0, 1)
    wq_partner.start()

    local_copies = [
        pltpu.make_async_copy(cells_ref.at[c], got.at[c, t, q], local_sems.at[0]),
        pltpu.make_async_copy(cond_ref, conds.at[c], local_sems.at[1]),
        pltpu.make_async_copy(wqkv_ref.at[mine], wq.at[mine], local_sems.at[2]),
        pltpu.make_async_copy(wout_ref, wo.at[t, c, q], local_sems.at[3]),
    ]
    for copy in local_copies:
        copy.start()
    blank = jnp.zeros((window, head_dim, nt * LANES), f32)
    k_rows[:window] = blank
    v_rows[:window] = blank
    k_rows[total + window :] = blank
    v_rows[total + window :] = blank
    thin = jnp.zeros((window, 1, nt * LANES), f32)
    for ref in (key_scale, value_scale):
        ref[:window] = thin
        ref[total + window :] = thin
    for copy in local_copies:
        copy.wait()
    cond_copy.wait()
    row_ids = lax.broadcasted_iota(jnp.int32, (rows, 1), 0)
    base[...] = jnp.zeros((rows, width), f32)
    base[:chans] = embed_ref[...].astype(f32)
    base[chans : chans + 1] = conds[0]
    base[chans + 1 : chans + 2] = conds[1]
    plain = base[...]
    centered = plain - jnp.mean(plain, axis=1, keepdims=True)
    gram = lax.dot_general(
        centered,
        centered,
        (((1,), (1,)), ((), ())),
        precision=HIGH,
        preferred_element_type=f32,
    ) * (1.0 / width)

    @pl.when(leads)
    def _():
        pass

    @pl.when(jnp.logical_not(leads))
    def _():
        for dc in range(nc):
            wqz_copy(1, dc).start()

    @pl.when(leads)
    def _():
        woz_copy(1).start()
        for p in range(2, pieces):
            woz_copy(p).start()

    wqz_copy(3, 0).wait_recv()
    wqy_copy(3, s).start()
    for copy in lat_copies:
        copy.wait()
    lat_forward.start()
    wox_copy(0).start()
    woc_copy(0, 0).start()
    lat_forward.wait()

    extra = lax.broadcasted_iota(jnp.int32, (chans, LANES), 0)
    lane = lax.broadcasted_iota(jnp.int32, (chans, LANES), 1)
    first = (extra == 0) & (lane < tok_count)
    second = (extra == 1) & (lane >= tok_count) & (lane < 2 * tok_count)
    marks = jnp.where(first | second, 1.0, 0.0)

    def unpack(i, carry):
        for side in range(nt):
            block = got[lax.rem(i, nc), side, i // nc].astype(f32)
            for h in range(2):
                tokens = block[:, h * tok_count : (h + 1) * tok_count]
                spread = jnp.concatenate([tokens, tokens, jnp.zeros((chans, gap), f32)], axis=1)
                flag = block[:, 2 * tok_count + h : 2 * tok_count + h + 1]
                cells[side, 2 * i + h, :chans] = spread.astype(bf16)
                cells[side, 2 * i + h, chans:] = (marks + flag).astype(bf16)
        return carry

    lax.fori_loop(0, total // 2, unpack, 0)

    level_column = cells[0, :, row_level, :].astype(f32)
    level_ids = lax.broadcasted_iota(jnp.int32, (total, LANES), 1).astype(f32)
    one_hot = (level_column == level_ids).astype(f32)[:, :levels_all]
    shift = jnp.dot(one_hot, mod_ref[0], precision=HIGH, preferred_element_type=f32)
    scale = jnp.dot(one_hot, mod_ref[1], precision=HIGH, preferred_element_type=f32) + 1.0
    is_shift = (row_ids == chans + 2) | (row_ids == chans + 3)
    for f in range(total):
        block = jnp.where(is_shift, shift[f : f + 1], centered * scale[f : f + 1])
        high, low = split2(block)
        scaled_hi[f * rows : (f + 1) * rows] = high
        scaled_lo[f * rows : (f + 1) * rows] = low

    group = LANES // rows

    def frame_cells(f):
        return jnp.concatenate([cells[i, f].astype(f32) for i in range(nt)], axis=1)

    def prepare(f, carry):
        cell = jnp.where(row_ids < chans + 2, frame_cells(f), 0.0)
        spread = jnp.sum(
            cell * jnp.dot(gram, cell, precision=HIGH, preferred_element_type=f32),
            axis=0,
            keepdims=True,
        )
        spread = jnp.maximum(spread, 0.0) + EPS_NORM
        inverse = lax.rsqrt(spread)
        sigma = spread * inverse
        sigma_hi = sigma.astype(bf16).astype(f32)
        cell = jnp.where(row_ids == chans + 2, sigma_hi, cell)
        cell = jnp.where(row_ids == chans + 3, sigma - sigma_hi, cell)
        low_row = pl.multiple_of(lax.rem(f, group) * rows, rows)
        inputs[f, pl.ds(low_row, rows)] = cell.astype(bf16)
        inputs[f, pl.ds(low_row + LANES, rows)] = cell.astype(bf16)
        value_scale[f + window] = inverse
        return carry

    lax.fori_loop(0, total // 2, prepare, 0, unroll=4)
    wqz_copy(2, 0).wait_recv()
    wqy_copy(2, s).start()
    lax.fori_loop(total // 2, total, prepare, 0, unroll=4)
    arrive_x(0)


    arrive(1)
    own_lanes = 2 * tok_count
    rest_lanes = 2 * own_lanes - LANES
    tail = att_out.shape[2] - head_dim
    lane_ids = lax.broadcasted_iota(jnp.int32, (1, LANES), 1)
    own_lane = lane_ids < own_lanes
    rest_lane = lane_ids < rest_lanes

    def join(low, high):
        rest = pltpu.roll(high, own_lanes, 1)
        return jnp.concatenate([jnp.where(own_lane, low, rest), rest], axis=1)

    own = join(*[cells[t, mine * per_core + i].astype(f32) for i in range(per_core)])
    embed_rows[...] = dot00(plain, jnp.where(row_ids < chans + 2, own, 0.0), HIGH)
    own_level = own[row_level : row_level + 1]
    own_hot = (
        own_level == lax.broadcasted_iota(jnp.int32, (levels_all, 1), 0).astype(f32)
    ).astype(f32)
    gate_rows[...] = dot00(mod_ref[2], own_hot, HIGH)

    wq_partner.wait()
    for k in (3, 2):
        wqy_copy(k, 1 - s).wait_recv()
    near_copy(0).wait_recv()
    near_copy(1).wait_recv()
    weights = wq[...].reshape(width, wq.shape[2])
    proj[...] = jnp.dot(scaled_hi[...], weights, preferred_element_type=f32) + jnp.dot(
        scaled_lo[...], weights, preferred_element_type=f32
    )

    diagonal = lax.broadcasted_iota(jnp.int32, (head_dim, head_dim), 0) == (
        lax.broadcasted_iota(jnp.int32, (head_dim, head_dim), 1)
    )

    def column(gain_ref):
        return jnp.sum(jnp.where(diagonal, gain_ref[...], 0.0), axis=1, keepdims=True)

    gain = column(query_gain_ref) * column(key_gain_ref) * head_dim**-0.5
    for g in range(total // group):
        block = proj[g * LANES : (g + 1) * LANES].T
        high, low = split2(block)
        proj_t[g] = jnp.concatenate([high, low], axis=1)

    def project(f, carry):
        whole = jnp.dot(proj_t[f // group], inputs[f], preferred_element_type=f32)
        inverse = value_scale[f + window]
        query = whole[:head_dim]
        key = whole[head_dim : 2 * head_dim]

        def rms(part):
            spread = jnp.mean(part * part, axis=0, keepdims=True)
            return inverse * lax.rsqrt(spread * inverse * inverse + EPS_NORM)

        q_rows[f] = query * gain * rms(query)
        k_rows[f + window] = key
        key_scale[f + window] = rms(key)
        v_rows[f + window] = whole[2 * head_dim : 3 * head_dim]
        return carry

    lax.fori_loop(0, total // 2, project, 0, unroll=8)
    arrive(2)
    lax.fori_loop(total // 2, total, project, 0, unroll=8)
    arrive_x(1)
    arrive(3)
    def attend(pair):
        done = []
        for inner in range(per_core):
            f = pair * per_core + inner
            cell = frame_cells(f)
            query = q_rows[f]
            numerator = jnp.zeros((head_dim, nt * LANES), f32)
            denominator = jnp.zeros((1, nt * LANES), f32)
            for o in range(span):
                score = jnp.sum(query * k_rows[f + o], axis=0, keepdims=True)
                row = row_level + 1 + o
                weight = jnp.exp(score * key_scale[f + o]) * cell[row : row + 1]
                numerator = numerator + (weight * value_scale[f + o]) * v_rows[f + o]
                denominator = denominator + weight
            done.append(numerator / denominator)
        for i in range(nt):
            low, high = (d[:, i * LANES : (i + 1) * LANES] for d in done)
            rest = pltpu.roll(high, own_lanes, 1)
            joined = jnp.where(own_lane, low, rest)
            upper = pltpu.roll(rest[head_dim - tail :], rest_lanes, 1)
            folded = jnp.where(rest_lane, rest[:tail], upper)
            att_out[pair, i] = jnp.concatenate([joined, folded], axis=0).astype(bf16)

    head = t * pairs + mine

    def att_copy(step, dt):
        pair = lax.rem(mine + step, pairs)
        other = lax.rem(t + dt, nt)
        return pltpu.make_async_remote_copy(
            src_ref=att_out.at[pair, other],
            dst_ref=att_in.at[head],
            send_sem=att_sems.at[0, step, dt],
            recv_sem=att_sems.at[1, step, dt],
            device_id={"queue": pair // nc, "tok": other, "cfg": lax.rem(pair, nc)},
            device_id_type=pl.DeviceIdType.MESH,
        )

    def attend_step(step, carry):
        attend(lax.rem(mine + step, pairs))
        for dt in range(nt):
            att_copy(step, dt).start()
        return carry

    lax.fori_loop(1, pairs, attend_step, 0, unroll=pairs - 1)
    attend(mine)
    for dt in range(1, nt):
        att_copy(0, dt).start()
    att_in[head] = att_out[mine, t]

    arrive_x(2)
    arrive_x(3)

    def att_wait(step, carry):
        for dt in range(nt):
            att_copy(step, dt).wait()
        return carry

    lax.fori_loop(1, pairs, att_wait, 0)
    for dt in range(1, nt):
        att_copy(0, dt).wait()
    for p in range(pieces):
        woc_copy(0, p).wait()
        woc_copy(1, p).wait()
    for p in range(pieces):
        if p not in shared:
            wox_copy(p).wait_send()

    group = pairs * head_dim
    arrived = att_in[...].astype(f32)
    folded = arrived[:, head_dim:]
    upper = pltpu.roll(folded[:, 2 * tail - head_dim :], LANES - rest_lanes, 2)
    attended = jnp.concatenate(
        [arrived[:, :head_dim], jnp.concatenate([folded, upper], axis=1)], axis=2
    )
    attended = attended.reshape(nt * group, 2 * LANES).astype(bf16)
    slices = []
    for i in range(nt):
        by_core = [
            jnp.dot(
                wo[i, k].reshape(nq * wo.shape[3], group),
                attended[i * group : (i + 1) * group],
                preferred_element_type=f32,
            )
            for k in range(nc)
        ]
        slices.append(by_core)
    piece = wo.shape[3]
    mixed = jnp.concatenate(
        [
            sum(slices[i][k][j * piece : (j + 1) * piece] for i in range(nt))
            for j in range(nq)
            for k in range(nc)
        ],
        axis=0,
    )
    summed = embed_rows[...] + gate_rows[...] * mixed
    deviate = summed - jnp.mean(summed, axis=0, keepdims=True)
    inverse = lax.rsqrt(jnp.mean(deviate * deviate, axis=0, keepdims=True) + EPS_NORM)
    rounded = deviate.astype(bf16)
    final_hi, final_lo = split2(
        wfinal_ref[...].astype(f32)
        * jnp.concatenate([final_gain_ref[i : i + 1] for i in range(width // LANES)], axis=1)
    )
    velocity = (
        jnp.dot(final_hi, rounded, preferred_element_type=f32)
        + jnp.dot(final_lo, rounded, preferred_element_type=f32)
    ) * inverse

    guidance = jnp.float32(0.0)
    for i in range(entries):
        guidance = guidance + jnp.where(index_ref[0] == i, table_ref[i], 0.0)

    def step_of(level):
        upcoming = noise_sigma(level / levels_all)
        current = noise_sigma((level + 1.0) / levels_all)
        return upcoming - current

    half = chans // nc
    for i in range(per_core):
        begin = i * own_lanes
        cond_vel = velocity[:, begin : begin + tok_count]
        uncond_vel = velocity[:, begin + tok_count : begin + 2 * tok_count]
        guided = uncond_vel + guidance * (cond_vel - uncond_vel)
        for k in range(nc):
            vel_half[k, i] = guided[k * half : (k + 1) * half]
        if i == 0:
            change = step_of(own_level[:, :tok_count])
            updated = latents_ref[0] + change * guided
            for k in range(nc):
                head_half[k] = updated[k * half : (k + 1) * half]

    own_slot = pl.ds(c * per_core, per_core)
    vel_copy = remote(vel_half.at[1 - c], vel_got, end_sems, (0,), 0, 0, 1)
    vel_copy.start()

    def head_copy(k):
        return pltpu.make_async_remote_copy(
            src_ref=head_half.at[k],
            dst_ref=head_got,
            send_sem=end_sems.at[0, 1 + k],
            recv_sem=end_sems.at[1, 1],
            device_id={"queue": lax.rem(q + nq - 1, nq), "cfg": k},
            device_id_type=pl.DeviceIdType.MESH,
        )

    @pl.when((c == 0) & (q > 0))
    def _():
        for k in range(nc):
            head_copy(k).start()

    guided_ref[own_slot] = vel_half[c]
    vel_copy.wait()
    guided_ref[pl.ds((1 - c) * per_core, per_core)] = vel_got[...]
    own_half = pl.ds(pl.multiple_of(c * half, half), half)
    for f in range(1, frames):
        level = cells[t, q * frames + f].astype(f32)[row_level : row_level + 1, :tok_count]
        queue_ref[f - 1] = latents_ref[f, own_half] + step_of(level) * guided_ref[f]

    @pl.when(q == nq - 1)
    def _():
        queue_ref[frames - 1] = noise_ref[...]

    @pl.when(q < nq - 1)
    def _():
        head_copy(0).wait_recv()
        queue_ref[frames - 1] = head_got[...]

    @pl.when((c == 0) & (q > 0))
    def _():
        for k in range(nc):
            head_copy(k).wait_send()

    for k in (3, 2):
        wqy_copy(k, s).wait_send()

    @pl.when(jnp.logical_not(leads))
    def _():
        for dc in range(nc):
            wqz_copy(1, dc).wait_send()

    @pl.when(leads)
    def _():
        for k in range(1, nq):
            for dc in range(nc):
                wqz_copy(k, dc).wait_send()
        for p in range(1, pieces):
            woz_copy(p).wait_send()
            woy_copy(0, p).wait_send()
            if p in shared:
                wox_copy(p).wait_send()
                woy_copy(1, p).wait_send()


def hand_on(guided_ref, queue_ref, guided_out, queue_out):
    guided_out[...] = guided_ref[...]
    queue_out[...] = queue_ref[...]


def on_device(
    latents,
    fresh_noise,
    levels,
    window_mask,
    cond_embed,
    level_mod,
    embed_weight,
    qkv_weight,
    query_gain,
    key_gain,
    out_weight,
    final_gain,
    final_weight,
    guide_table,
    guide_index,
):
    frames, chans, tok_count = latents.shape
    width = embed_weight.shape[1]
    head_dim = query_gain.shape[0]
    levels_all = level_mod.shape[0]
    nq, nt, nc = (lax.axis_size(a) for a in ("queue", "tok", "cfg"))
    shard_rows, _, local_cols = qkv_weight.shape
    pairs = nq * nc
    span = window_mask.shape[1]
    window = span // 2
    rows = 2 * chans
    fits = (
        local_cols == pairs * head_dim
        and frames % nc == 0
        and frames % 2 == 0
        and chans >= 5 + span
        and 2 * tok_count + 2 <= LANES
        and nc == 2
        and nt == 2
        and lax.axis_size("scene") == 2
        and chans % (8 * nc) == 0
        and 2 * tok_count <= LANES
        and levels_all <= LANES
        and nq == 4
        and width % LANES == 0
        and frames == 2 * nc
        and 4 * tok_count == LANES + LANES // 2
        and frames == LANES // rows
    )
    if not fits:
        return on_device_plain(
            latents, fresh_noise, levels, window_mask, cond_embed, level_mod, embed_weight,
            qkv_weight, query_gain, key_gain, out_weight, final_gain, final_weight,
            guide_table, guide_index,
        )
    f32, bf16 = jnp.float32, jnp.bfloat16
    packed = -(-3 * head_dim // LANES) * LANES
    wqkv = qkv_weight.transpose(1, 0, 2)
    wout = out_weight.T
    wfinal = final_weight.T
    mods = level_mod.transpose(1, 0, 2)
    total = nq * frames
    per_core = frames // nc
    half = chans // nc
    tail = -(-head_dim // 16) * 8
    dims = (nq, nt, nc, frames, chans, head_dim, window, tok_count, guide_table.shape[0])
    vmem = pl.BlockSpec(memory_space=pltpu.VMEM)
    smem = pl.BlockSpec(memory_space=pltpu.SMEM)
    dma = pltpu.SemaphoreType.DMA
    out = jax.ShapeDtypeStruct((frames, half, tok_count), f32)
    staged = [
        cond_embed, mods, embed_weight, wqkv, query_gain[None], key_gain[None], wout,
        final_gain.reshape(width // LANES, LANES), wfinal, latents, fresh_noise,
    ]
    scalars = [guide_table, guide_index, levels, window_mask]
    anywhere = pl.BlockSpec(memory_space=pl.ANY)
    results = pl.pallas_call(
        functools.partial(staged_kernel, dims, len(staged), len(scalars)),
        out_shape=(out, out),
        in_specs=[anywhere] * len(staged) + [smem] * len(scalars),
        out_specs=(vmem, vmem),
        scratch_shapes=[
            *[pltpu.VMEM(array.shape, array.dtype) for array in staged],
            dma((len(staged),)),
            pltpu.VMEM((frames // 2, chans, LANES), bf16),
            pltpu.VMEM((pairs, shard_rows, packed), bf16),
            pltpu.VMEM((nc, nt, nq, chans, LANES), bf16),
            pltpu.VMEM((nt, total, rows, LANES), bf16),
            pltpu.VMEM((total, 2 * LANES, nt * LANES), bf16),
            pltpu.VMEM((total + 2 * window, 1, nt * LANES), f32),
            pltpu.VMEM((total + 2 * window, 1, nt * LANES), f32),
            pltpu.VMEM((total * rows // LANES, packed, 2 * LANES), bf16),
            pltpu.VMEM((width, per_core * LANES), f32),
            pltpu.VMEM((width, per_core * LANES), f32),
            pltpu.VMEM((nc, 1, width), f32),
            pltpu.VMEM((rows, width), f32),
            pltpu.VMEM((pairs, shard_rows, packed), bf16),
            pltpu.VMEM((nt, nc, nq, wout.shape[0], wout.shape[1]), bf16),
            pltpu.VMEM((total * rows, width), bf16),
            pltpu.VMEM((total * rows, width), bf16),
            pltpu.VMEM((total * rows, packed), f32),
            pltpu.VMEM((total, head_dim, nt * LANES), f32),
            pltpu.VMEM((total + 2 * window, head_dim, nt * LANES), f32),
            pltpu.VMEM((total + 2 * window, head_dim, nt * LANES), f32),
            pltpu.VMEM((pairs, nt, head_dim + tail, LANES), bf16),
            pltpu.VMEM((nt * pairs, head_dim + tail, LANES), bf16),
            pltpu.VMEM((nc, per_core, half, tok_count), f32),
            pltpu.VMEM((per_core, half, tok_count), f32),
            pltpu.VMEM((nc, half, tok_count), f32),
            pltpu.VMEM((half, tok_count), f32),
            dma((2, nq, nt)),
            dma((2, 1)),
            dma((2, 1)),
            dma((2, nq, nc)),
            dma((2, nq)),
            dma((2, nq + 1)),
            dma((2, 2, nq)),
            dma((2, nq)),
            dma((2, 2, nq)),
            dma((2, pairs, nt)),
            dma((2, 1 + nc)),
            dma((4,)),
        ],
        compiler_params=pltpu.CompilerParams(collective_id=0, has_side_effects=True),
    )(
        *staged, *scalars
    )
    return pl.pallas_call(
        hand_on,
        out_shape=(out, out),
        in_specs=[vmem, vmem],
        out_specs=(vmem, vmem),
        scratch_shapes=[],
    )(*results)


def solution(mesh):
    placed = (
        P(("scene", "queue"), None, "tok"),
        P(("scene", "cfg"), "tok"),
        P(("scene", "queue")),
        P(("scene", "queue"), None),
        P(("scene", "cfg"), None),
        P(),
        P(),
        P(("queue", "cfg"), None, "tok"),
        P(),
        P(),
        P("tok", ("queue", "cfg")),
        P(),
        P(),
        P(),
        P(),
    )
    return jax.shard_map(
        on_device,
        mesh=mesh,
        in_specs=placed,
        out_specs=(P(("scene", "queue"), "cfg", "tok"), P(("scene", "queue"), "cfg", "tok")),
        check_vma=False,
    )
```
